128 devices in a mesh: dp: 32 (over y, z, core), expert: 4 (over x).
Axes of the slice: x: 4, y: 4, z: 4, core: 2. Of those that a mesh axis runs over, the one named last changes fastest.
Arguments:
- local_grads: bfloat16 [4, 32, 1024, 3584], P('expert', 'dp')
- momentum: float32 [4, 1024, 3584], P('expert', None, 'dp'), may hold values from -6 to 6
Outputs:
- new_momentum: float32 [4, 1024, 3584], P('expert', None, 'dp')
- update: float32 [4, 1024, 3584], P('expert', None, 'dp')
The draws below stay inside these ranges and needn't reach their ends.
All inputs are finite; a program needn't handle non-finite values.
Results may differ from the reference program's by a relative error of at most 0.0003.
Values sent between devices are 32-bit elements; how exact they have to be, the bound alone decides.
A program may use at most 128 MiB of HBM per device.

```python
import math
import jax
import jax.numpy as jnp
from jax import lax

HID = 1024
WID = 3584
ITERS = 3
GROUPS = 4
REPLICAS = 32


def draw_local_grads(key, part):
    keys = jax.random.split(jax.random.fold_in(key, 17), 3)
    top_row = 10.0
    row_scale = jnp.exp(jax.random.uniform(keys[0], (GROUPS, 1, HID, 1), jnp.float32) * math.log(top_row))
    col_scale = jnp.exp(jax.random.uniform(keys[1], (GROUPS, 1, 1, WID), jnp.float32) * math.log(10.0))
    col_ramp = jnp.exp(jnp.arange(WID, dtype=jnp.float32) / max(WID - 1, 1) * math.log(3.0))
    group_ramp = jnp.exp(jnp.arange(GROUPS, dtype=jnp.float32) / max(GROUPS - 1, 1) * math.log(3.0))
    shaped = row_scale * col_scale * col_ramp[None, None, None, :] * group_ramp[:, None, None, None] * 0.05
    values = jax.random.normal(keys[2], (GROUPS, REPLICAS, HID, WID), jnp.float32)
    return (values * shaped).astype(jnp.bfloat16)


def block_scale(own_key, shape, cuts, low, high):
    level = 1.0
    for dim, blocks in cuts:
        steps = jax.random.uniform(jax.random.fold_in(jax.random.fold_in(own_key, 6), dim), (blocks,), jnp.float32, low / len(cuts), high / len(cuts))
        level = level * jnp.repeat(jnp.exp(steps), shape[dim] // blocks).reshape((-1,) + (1,) * (len(shape) - 1 - dim))
    return level


def gaussian(key, shape, spread, limit, shards=(), held_as=jnp.bfloat16):
    array = jax.random.normal(key, shape, jnp.float32) * spread
    if len(shards) > 0:
        array = block_scale(key, shape, shards, -0.22, 0.18) * array
    return jnp.clip(array, min=-limit, max=limit).astype(held_as)


def setup_inputs(seed: int = 0) -> dict:
    splits = jax.random.split(jax.random.key(seed), 3)
    return {
        "local_grads": draw_local_grads(jax.random.fold_in(splits[2], 71), 0),
        "momentum": gaussian(splits[1], (GROUPS, HID, WID), 1.0, 6.0, ((0, 4), (2, 32)), jnp.float32),
    }


first_coef = 3.4445
second_coef = -4.775
third_coef = 2.0315
momentum_decay = 0.95

def precise(left, right):
    return jnp.dot(left, right, precision=lax.Precision.HIGHEST, preferred_element_type=jnp.float32)

def orthogonal(blend):
    iterate = blend / (jnp.sqrt(jnp.sum(blend * blend)) + 1e-07)
    for number in range(ITERS):
        gram = precise(iterate, iterate.T)
        poly = second_coef * gram + third_coef * precise(gram, gram)
        iterate = first_coef * iterate + precise(poly, iterate)
    return iterate * (0.2 * math.sqrt(max(HID, WID)))

def reference(local_grads, momentum):
    grads = lax.optimization_barrier(jnp.sum(local_grads, axis=1, dtype=jnp.float32))
    root_mean = jnp.sqrt(jnp.mean(grads * grads) + 1e-06)
    factor = jnp.minimum(1.0, 1.0 / root_mean)
    clipped = factor * grads
    new_momentum = momentum_decay * momentum + clipped
    blend = clipped + momentum_decay * new_momentum
    update = lax.map(orthogonal, blend)
    return (new_momentum, update)
```

```python
import math

import jax
import jax.numpy as jnp
from jax import lax
from jax.experimental import pallas as pl
from jax.experimental.pallas import tpu as pltpu
from jax.sharding import Mesh
from jax.sharding import PartitionSpec as P

MESH = pl.DeviceIdType.MESH
HID, WID = 1024, 3584
OWN = WID // 32
HALF = OWN // 2
LANES = HID // 2
ORDER = (2, 1, 3, 0)
DP = ("dp_0", "dp_1", "dp_2")
DP_EXPERT = DP + ("expert",)

first_coef = 3.4445
second_coef = -4.775
third_coef = 2.0315
momentum_decay = 0.95


def place():
    return [lax.axis_index(a) for a in ("dp_0", "dp_1", "dp_2", "expert")]


def reduce_scatter_kernel(x_hbm, out, raw, flat, mine, pa, pb, ra, rb, qa, qb, r2, load_sem, send_sem, recv_sem):
    y, z, c, x = place()
    partner = (y, z, 1 - c, x)
    y_next, y_prev = (lax.rem(y + 1, 4), z, c, x), (lax.rem(y + 3, 4), z, c, x)
    z_next, z_prev = (y, lax.rem(z + 1, 4), c, x), (y, lax.rem(z + 3, 4), c, x)
    loads = []
    for k in range(4):
        first = pl.multiple_of(lax.rem(y + ORDER[k], 4) * 896, 128)
        load = pltpu.make_async_copy(x_hbm.at[:, pl.ds(first, 896)], raw.at[k], load_sem.at[k])
        load.start()
        loads.append(load)
    barrier = pltpu.get_barrier_semaphore()
    for peer in (partner, y_next, y_prev, z_next, z_prev):
        pl.semaphore_signal(barrier, inc=1, device_id=peer, device_id_type=MESH)
    pl.semaphore_wait(barrier, 5)

    started = []

    def send(src, dst, peer):
        n = len(started)
        copy = pltpu.make_async_remote_copy(
            src_ref=src, dst_ref=dst, send_sem=send_sem.at[n], recv_sem=recv_sem.at[n],
            device_id=peer, device_id_type=MESH)
        copy.start()
        started.append(copy)
        return copy

    row = lax.broadcasted_iota(jnp.int32, (128, 128), 0)
    col = lax.broadcasted_iota(jnp.int32, (128, 128), 1)
    eye = jnp.where(row == col, 1.0, 0.0).astype(jnp.bfloat16)

    def turn(k):
        loads[k].wait()
        for b in range(7):
            flat[k, 128 * b:128 * b + 128, :] = lax.dot_general(
                eye, raw[k, :, 128 * b:128 * b + 128], (((1,), (1,)), ((), ())),
                preferred_element_type=jnp.float32)

    def rows_of(j, core):
        return pl.multiple_of((lax.rem(z + ORDER[j], 4) * 2 + core) * OWN, 8)

    pair = {}

    def exchange(k):
        for j in range(4):
            pair[k, j] = send(flat.at[k, pl.ds(rows_of(j, 1 - c), OWN)], mine.at[k, j], partner)

    def pair_sum(k):
        for j in range(4):
            pair[k, j].wait_recv()
            base = rows_of(j, c)
            for h in range(2):
                lanes = slice(LANES * h, LANES * h + LANES)
                pa[k, j, h] = flat[k, pl.ds(base, HALF), lanes] + mine[k, j, 0:HALF, lanes]
                pb[j, k, h] = flat[k, pl.ds(base + HALF, HALF), lanes] + mine[k, j, HALF:OWN, lanes]

    def relay(p, r, nxt, prv):
        return [send(p(0, 0), r.at[0], nxt), send(p(0, 1), r.at[1], prv)]

    def unmerged_next(p, r, nxt):
        return send(p(1, 1), r.at[2], nxt)

    def unmerged_prev(p, r, prv):
        return send(p(2, 0), r.at[3], prv)

    def merged(p, r, nxt, prv, relays):
        relays[0].wait_recv()
        p(1, 0)[...] += r[0]
        first = send(p(1, 0), r.at[4], nxt)
        relays[1].wait_recv()
        p(2, 1)[...] += r[1]
        return [first, send(p(2, 1), r.at[5], prv)]

    def total(p, r, parts):
        for part in parts:
            part.wait_recv()
        return p(3, 0)[...] + r[4] + r[3], p(3, 1)[...] + r[2] + r[5]

    a_slots = [lambda s, h, j=j: pa.at[s, j, h] for j in range(4)]
    b_slots = [lambda s, h, k=k: pb.at[s, k, h] for k in range(4)]
    a_sent, b_sent = [[] for _ in range(4)], [[] for _ in range(4)]
    a_relay, b_relay = [None] * 4, [None] * 4

    def launch(k):
        pair_sum(k)
        b_relay[k] = relay(b_slots[k], rb.at[k], z_next, z_prev)
        if k == 0:
            for j in range(4):
                a_relay[j] = relay(a_slots[j], ra.at[j], y_next, y_prev)
        b_sent[k] += [unmerged_next(b_slots[k], rb.at[k], z_next), unmerged_prev(b_slots[k], rb.at[k], z_prev)]
        if k == 1:
            for j in range(4):
                a_sent[j].append(unmerged_next(a_slots[j], ra.at[j], y_next))
        if k == 2:
            for j in range(4):
                a_sent[j].append(unmerged_prev(a_slots[j], ra.at[j], y_prev))

    turn(0)
    exchange(0)
    turn(1)
    exchange(1)
    launch(0)
    turn(2)
    exchange(2)
    launch(1)
    turn(3)
    exchange(3)
    launch(2)
    launch(3)
    for i in range(4):
        a_sent[i] += merged(a_slots[i], ra.at[i], y_next, y_prev, a_relay[i])
        b_sent[i] += merged(b_slots[i], rb.at[i], z_next, z_prev, b_relay[i])

    last_a, last_b = (lambda s, h: qa.at[s, h]), (lambda s, h: qb.at[s, h])
    a_last, b_last = [], []
    for i in range(4):
        for q, slots, r, sent in ((qa, a_slots, ra, a_sent), (qb, b_slots, rb, b_sent)):
            q[i, 0], q[i, 1] = total(slots[i], r.at[i], sent[i])
        for last, r, nxt, prv, kept in ((last_a, r2.at[0], z_next, z_prev, a_last), (last_b, r2.at[1], y_next, y_prev, b_last)):
            if i == 0:
                kept.append(relay(last, r, nxt, prv))
            if i == 1:
                kept.append(unmerged_next(last, r, nxt))
            if i == 2:
                kept.append(unmerged_prev(last, r, prv))
    a_last += merged(last_a, r2.at[0], z_next, z_prev, a_last[0])
    b_last += merged(last_b, r2.at[1], y_next, y_prev, b_last[0])
    out[0:HALF, 0:LANES], out[0:HALF, LANES:HID] = total(last_a, r2.at[0], a_last[1:])
    out[HALF:OWN, 0:LANES], out[HALF:OWN, LANES:HID] = total(last_b, r2.at[1], b_last[1:])
    for copy in started:
        copy.wait_send()


COPIES = 16 + 48 + 12


def reduce_scatter(local):
    piece = (HALF, LANES)
    return pl.pallas_call(
        reduce_scatter_kernel,
        out_shape=jax.ShapeDtypeStruct((OWN, HID), jnp.float32),
        in_specs=[pl.BlockSpec(memory_space=pl.ANY)],
        out_specs=pl.BlockSpec(memory_space=pltpu.VMEM),
        scratch_shapes=[
            pltpu.VMEM((4, HID, 896), jnp.bfloat16),
            pltpu.VMEM((4, 896, HID), jnp.float32),
            pltpu.VMEM((4, 4, OWN, HID), jnp.float32),
            pltpu.VMEM((4, 4, 2) + piece, jnp.float32),
            pltpu.VMEM((4, 4, 2) + piece, jnp.float32),
            pltpu.VMEM((4, 6) + piece, jnp.float32),
            pltpu.VMEM((4, 6) + piece, jnp.float32),
            pltpu.VMEM((4, 2) + piece, jnp.float32),
            pltpu.VMEM((4, 2) + piece, jnp.float32),
            pltpu.VMEM((2, 6) + piece, jnp.float32),
            pltpu.SemaphoreType.DMA((4,)),
            pltpu.SemaphoreType.DMA((COPIES,)),
            pltpu.SemaphoreType.DMA((COPIES,)),
        ],
        compiler_params=pltpu.CompilerParams(collective_id=0, has_side_effects=True, vmem_limit_bytes=60 << 20),
        name="sum_gradients",
    )(local)


def precise(left, right):
    return jnp.dot(left, right, precision=lax.Precision.HIGHEST, preferred_element_type=jnp.float32)


def body(local_grads, momentum):
    grads = reduce_scatter(local_grads[0, 0])
    total_sq = lax.psum(jnp.sum(grads * grads), DP_EXPERT)
    root_mean = jnp.sqrt(total_sq / (HID * WID * lax.axis_size("expert")) + 1e-06)
    clipped = jnp.minimum(1.0, 1.0 / root_mean) * grads
    new_momentum = momentum_decay * momentum[0].T + clipped
    blend = clipped + momentum_decay * new_momentum
    gram = lax.psum(precise(blend.T, blend), DP)
    norm = jnp.sqrt(jnp.trace(gram)) + 1e-07
    iterate = blend / norm
    gram = gram / (norm * norm)
    lower = second_coef * gram + third_coef * precise(gram, gram)
    left = first_coef * gram + precise(gram, lower)
    gram1 = first_coef * left + precise(left, lower)
    lower1 = second_coef * gram1 + third_coef * precise(gram1, gram1)

    def step1(value):
        return first_coef * value + precise(value, lower1)

    def gram2(value):
        return step1(precise(step1(value), gram1))

    iterate = step1(first_coef * iterate + precise(iterate, lower))
    product = gram2(iterate)
    iterate = first_coef * iterate + gram2(second_coef * iterate + third_coef * product)
    update = iterate * (0.2 * math.sqrt(max(HID, WID)))
    return (new_momentum.T[None], update.T[None])


def solution(mesh):
    finer = Mesh(mesh.devices.reshape(4, 4, 2, mesh.shape["expert"]), DP_EXPERT)
    in_specs = (P("expert", DP, None, None), P("expert", None, DP))
    out_specs = (P("expert", None, DP), P("expert", None, DP))
    return jax.shard_map(body, mesh=finer, in_specs=in_specs, out_specs=out_specs, check_vma=False)
```

```python
import functools
import math

import jax
import jax.numpy as jnp
from jax import lax
from jax.experimental import pallas as pl
from jax.experimental.pallas import tpu as pltpu
from jax.sharding import Mesh
from jax.sharding import PartitionSpec as P

MESH = pl.DeviceIdType.MESH
HID, WID = 1024, 3584
OWN = WID // 32
HALF = OWN // 2
LANES = HID // 2
ORDER = (2, 1, 3, 0)
DP = ("dp_0", "dp_1", "dp_2")
DP_EXPERT = DP + ("expert",)


def place():
    return [lax.axis_index(a) for a in ("dp_0", "dp_1", "dp_2", "expert")]


def reduce_scatter_kernel(x_hbm, out, raw, flat, mine, pa, pb, ra, rb, qa, qb, r2, load_sem, send_sem, recv_sem):
    y, z, c, x = place()
    partner = (y, z, 1 - c, x)
    y_next, y_prev = (lax.rem(y + 1, 4), z, c, x), (lax.rem(y + 3, 4), z, c, x)
    z_next, z_prev = (y, lax.rem(z + 1, 4), c, x), (y, lax.rem(z + 3, 4), c, x)
    loads = []
    for k in range(4):
        first = pl.multiple_of(lax.rem(y + ORDER[k], 4) * 896, 128)
        load = pltpu.make_async_copy(x_hbm.at[:, pl.ds(first, 896)], raw.at[k], load_sem.at[k])
        load.start()
        loads.append(load)
    barrier = pltpu.get_barrier_semaphore()
    for peer in (partner, y_next, y_prev, z_next, z_prev):
        pl.semaphore_signal(barrier, inc=1, device_id=peer, device_id_type=MESH)
    pl.semaphore_wait(barrier, 5)

    started = []

    def send(src, dst, peer):
        n = len(started)
        copy = pltpu.make_async_remote_copy(
            src_ref=src, dst_ref=dst, send_sem=send_sem.at[n], recv_sem=recv_sem.at[n],
            device_id=peer, device_id_type=MESH)
        copy.start()
        started.append(copy)
        return copy

    row = lax.broadcasted_iota(jnp.int32, (128, 128), 0)
    col = lax.broadcasted_iota(jnp.int32, (128, 128), 1)
    eye = jnp.where(row == col, 1.0, 0.0).astype(jnp.bfloat16)

    def turn(k):
        loads[k].wait()
        for b in range(7):
            flat[k, 128 * b:128 * b + 128, :] = lax.dot_general(
                eye, raw[k, :, 128 * b:128 * b + 128], (((1,), (1,)), ((), ())),
                preferred_element_type=jnp.float32)

    def rows_of(j, core):
        return pl.multiple_of((lax.rem(z + ORDER[j], 4) * 2 + core) * OWN, 8)

    pair = {}

    def exchange(k):
        for j in range(4):
            pair[k, j] = send(flat.at[k, pl.ds(rows_of(j, 1 - c), OWN)], mine.at[k, j], partner)

    def pair_sum(k):
        for j in range(4):
            pair[k, j].wait_recv()
            base = rows_of(j, c)
            for h in range(2):
                lanes = slice(LANES * h, LANES * h + LANES)
                pa[k, j, h] = flat[k, pl.ds(base, HALF), lanes] + mine[k, j, 0:HALF, lanes]
                pb[j, k, h] = flat[k, pl.ds(base + HALF, HALF), lanes] + mine[k, j, HALF:OWN, lanes]

    def relay(p, r, nxt, prv):
        return [send(p(0, 0), r.at[0], nxt), send(p(0, 1), r.at[1], prv)]

    def unmerged_next(p, r, nxt):
        return send(p(1, 1), r.at[2], nxt)

    def unmerged_prev(p, r, prv):
        return send(p(2, 0), r.at[3], prv)

    def merged(p, r, nxt, prv, relays):
        relays[0].wait_recv()
        p(1, 0)[...] += r[0]
        first = send(p(1, 0), r.at[4], nxt)
        relays[1].wait_recv()
        p(2, 1)[...] += r[1]
        return [first, send(p(2, 1), r.at[5], prv)]

    def total(p, r, parts):
        for part in parts:
            part.wait_recv()
        return p(3, 0)[...] + r[4] + r[3], p(3, 1)[...] + r[2] + r[5]

    a_slots = [lambda s, h, j=j: pa.at[s, j, h] for j in range(4)]
    b_slots = [lambda s, h, k=k: pb.at[s, k, h] for k in range(4)]
    a_sent, b_sent = [[] for _ in range(4)], [[] for _ in range(4)]
    a_relay, b_relay = [None] * 4, [None] * 4

    def launch(k):
        pair_sum(k)
        b_relay[k] = relay(b_slots[k], rb.at[k], z_next, z_prev)
        if k == 0:
            for j in range(4):
                a_relay[j] = relay(a_slots[j], ra.at[j], y_next, y_prev)
        b_sent[k] += [unmerged_next(b_slots[k], rb.at[k], z_next), unmerged_prev(b_slots[k], rb.at[k], z_prev)]
        if k == 1:
            for j in range(4):
                a_sent[j].append(unmerged_next(a_slots[j], ra.at[j], y_next))
        if k == 2:
            for j in range(4):
                a_sent[j].append(unmerged_prev(a_slots[j], ra.at[j], y_prev))

    turn(0)
    exchange(0)
    turn(1)
    exchange(1)
    launch(0)
    turn(2)
    exchange(2)
    launch(1)
    turn(3)
    exchange(3)
    launch(2)
    launch(3)
    for i in range(4):
        a_sent[i] += merged(a_slots[i], ra.at[i], y_next, y_prev, a_relay[i])
        b_sent[i] += merged(b_slots[i], rb.at[i], z_next, z_prev, b_relay[i])

    last_a, last_b = (lambda s, h: qa.at[s, h]), (lambda s, h: qb.at[s, h])
    a_last, b_last = [], []
    for i in range(4):
        for q, slots, r, sent in ((qa, a_slots, ra, a_sent), (qb, b_slots, rb, b_sent)):
            q[i, 0], q[i, 1] = total(slots[i], r.at[i], sent[i])
        for last, r, nxt, prv, kept in ((last_a, r2.at[0], z_next, z_prev, a_last), (last_b, r2.at[1], y_next, y_prev, b_last)):
            if i == 0:
                kept.append(relay(last, r, nxt, prv))
            if i == 1:
                kept.append(unmerged_next(last, r, nxt))
            if i == 2:
                kept.append(unmerged_prev(last, r, prv))
    a_last += merged(last_a, r2.at[0], z_next, z_prev, a_last[0])
    b_last += merged(last_b, r2.at[1], y_next, y_prev, b_last[0])
    out[0:HALF, 0:LANES], out[0:HALF, LANES:HID] = total(last_a, r2.at[0], a_last[1:])
    out[HALF:OWN, 0:LANES], out[HALF:OWN, LANES:HID] = total(last_b, r2.at[1], b_last[1:])
    for copy in started:
        copy.wait_send()


COPIES = 16 + 48 + 12


def reduce_scatter(local):
    piece = (HALF, LANES)
    return pl.pallas_call(
        reduce_scatter_kernel,
        out_shape=jax.ShapeDtypeStruct((OWN, HID), jnp.float32),
        in_specs=[pl.BlockSpec(memory_space=pl.ANY)],
        out_specs=pl.BlockSpec(memory_space=pltpu.VMEM),
        scratch_shapes=[
            pltpu.VMEM((4, HID, 896), jnp.bfloat16),
            pltpu.VMEM((4, 896, HID), jnp.float32),
            pltpu.VMEM((4, 4, OWN, HID), jnp.float32),
            pltpu.VMEM((4, 4, 2) + piece, jnp.float32),
            pltpu.VMEM((4, 4, 2) + piece, jnp.float32),
            pltpu.VMEM((4, 6) + piece, jnp.float32),
            pltpu.VMEM((4, 6) + piece, jnp.float32),
            pltpu.VMEM((4, 2) + piece, jnp.float32),
            pltpu.VMEM((4, 2) + piece, jnp.float32),
            pltpu.VMEM((2, 6) + piece, jnp.float32),
            pltpu.SemaphoreType.DMA((4,)),
            pltpu.SemaphoreType.DMA((COPIES,)),
            pltpu.SemaphoreType.DMA((COPIES,)),
        ],
        compiler_params=pltpu.CompilerParams(collective_id=0, has_side_effects=True, vmem_limit_bytes=60 << 20),
        name="sum_gradients",
    )(local)


momentum_decay = 0.95
BLOCK = 128
PAIRS = (((0, 7), (3, 4)), ((1, 6), (2, 5)))
FIRST = 5


def halves(value):
    high = value.astype(jnp.bfloat16)
    return high, (value - high.astype(jnp.float32)).astype(jnp.bfloat16)


def gram_kernel(count, g_ref, m_ref, new_ref, start_ref, gram_ref, s1, s2, s3, both, bb, a0, a1, b0, b1, r0, r1, q0, q1, t0, t1, w00, w01, w10, w11, send_sem, recv_sem):
    y, z, c, x = place()
    partner = (y, z, 1 - c, x)
    line = x * 2 + c
    y_line = [(lax.rem(y + d, 4), z, c, x) for d in (1, 2, 3)]
    z_line = [(y, lax.rem(z + d, 4), c, x) for d in (1, 2, 3)]
    x_line = [(y, z, lax.rem(lax.rem(line + d, 8), 2), lax.rem(line + d, 8) // 2) for d in range(1, 8)]
    y_ring, z_ring = (y_line[0], y_line[2]), (z_line[0], z_line[2])
    barrier = pltpu.get_barrier_semaphore()
    for peer in x_line + y_line + z_line:
        pl.semaphore_signal(barrier, inc=1, device_id=peer, device_id_type=MESH)
    pl.semaphore_wait(barrier, 13)

    started = []

    def send(src, dst, peer):
        n = len(started)
        copy = pltpu.make_async_remote_copy(
            src_ref=src, dst_ref=dst, send_sem=send_sem.at[n], recv_sem=recv_sem.at[n],
            device_id=peer, device_id_type=MESH)
        copy.start()
        started.append(copy)
        return copy

    square = g_ref[0:8, :] * g_ref[0:8, :]
    for i in range(1, OWN // 8):
        square += g_ref[8 * i:8 * i + 8, :] * g_ref[8 * i:8 * i + 8, :]
    tile = square[:, 0:128]
    for i in range(1, 8):
        tile += square[:, 128 * i:128 * i + 128]
    for buf, own, peers in ((s1, line, x_line), (s2, y, y_line), (s3, z, z_line)):
        buf[own] = tile
        copies = [send(buf.at[own], buf.at[own], peer) for peer in peers]
        if buf is s1:
            pair = [send(g_ref, both.at[0], partner), send(m_ref, both.at[1], partner)]
        for copy in copies:
            copy.wait_recv()
        tile = buf[0]
        for i in range(1, buf.shape[0]):
            tile += buf[i]
    root_mean = jnp.sqrt(jnp.sum(tile, keepdims=True) / count + 1e-06)
    factor = jnp.minimum(1.0, 1.0 / root_mean)
    clipped = factor * g_ref[...]
    new = momentum_decay * m_ref[...] + clipped
    new_ref[...] = new
    blend = clipped + momentum_decay * new
    bb[0:OWN] = blend
    for copy in pair:
        copy.wait_recv()
    clipped = factor * both[0]
    bb[OWN:2 * OWN] = clipped + momentum_decay * (momentum_decay * both[1] + clipped)
    high, low = halves(bb[...])
    turned = bb[...].T
    turned_high, turned_low = halves(turned)

    def dot(left, right):
        return jnp.dot(left, right, preferred_element_type=jnp.float32)

    for core in range(2):
        @pl.when(c == core)
        def _(core=core):
            for (first, second), (u0, u1) in zip(PAIRS[core], ((a0, a1), (b0, b1))):
                swap = u0 is b0
                place_in = 0
                for b in (first, second):
                    lh, ll = turned_high[BLOCK * b:BLOCK * b + BLOCK], turned_low[BLOCK * b:BLOCK * b + BLOCK]
                    rh, rl = high[:, BLOCK * b:], low[:, BLOCK * b:]
                    rows = dot(lh, rh) + (dot(lh, rl) + dot(ll, rh))
                    for i in range(16):
                        dy, dz = lax.rem(i // 4 + 4 - y, 4), lax.rem(i % 4 + 4 - z, 4)
                        one, two = (dz, dy) if swap else (dy, dz)
                        for t in range(8 - b):
                            value = rows[8 * i:8 * i + 8, BLOCK * t:BLOCK * t + BLOCK]
                            n = place_in + t
                            if n < FIRST:
                                u0[one, two, n] = value
                            else:
                                u1[one, two, n - FIRST] = value
                    place_in += 8 - b

    def begin(p, r, ring):
        nxt, prv = ring
        relays = [send(p[0].at[2], r[0].at[0], nxt), send(p[1].at[2], r[1].at[0], prv)]
        return relays, [send(p[1].at[1], r[1].at[1], nxt), send(p[0].at[3], r[0].at[1], prv)]

    def merge(p, r, ring, relays):
        nxt, prv = ring
        relays[0].wait_recv()
        p[0][1] += r[0][0]
        copies = [send(p[0].at[1], r[0].at[2], nxt)]
        relays[1].wait_recv()
        p[1][3] += r[1][0]
        return copies + [send(p[1].at[3], r[1].at[2], prv)]

    def end(p, r, copies):
        for copy in copies:
            copy.wait_recv()
        return [p[h][0] + r[h][1] + r[h][2] for h in range(2)]

    def at(refs, i):
        return [ref.at[i] for ref in refs]

    def reduce(sets):
        begun = [begin(*s) for s in sets]
        merged = [merge(*s, relays) + copies for s, (relays, copies) in zip(sets, begun)]
        return [end(s[0], s[1], copies) for s, copies in zip(sets, merged)]

    first_phase = reduce((((a0, a1), at((r0, r1), 0), y_ring), ((b0, b1), at((r0, r1), 1), z_ring)))
    for i in range(2):
        q0[i], q1[i] = first_phase[i]
    second_phase = reduce(((at((q0, q1), 0), at((t0, t1), 0), z_ring), (at((q0, q1), 1), at((t0, t1), 1), y_ring)))

    ws = ((w00.at[c], w01.at[c]), (w10.at[c], w11.at[c]))
    for i in range(2):
        ws[i][0][0, 0], ws[i][1][0, 0] = second_phase[i]

    def gather(sets, seen):
        stage = []
        for p, (nxt, prv) in sets:
            stage.append([
                send(p[0].at[0], p[0].at[3], nxt), send(p[1].at[0], p[1].at[1], prv),
                send(p[1].at[0], p[1].at[3], nxt), send(p[0].at[0], p[0].at[1], prv)])
        relays = []
        for n, (p, (nxt, prv)) in enumerate(sets):
            stage[n][0].wait_recv()
            relays.append(send(p[0].at[3], p[0].at[2], nxt))
            stage[n][1].wait_recv()
            relays.append(send(p[1].at[1], p[1].at[2], prv))
            seen(n, (0, 3))
            seen(n, (1, 1))
        for n in range(2):
            stage[n][2].wait_recv()
            seen(n, (1, 3))
            stage[n][3].wait_recv()
            seen(n, (0, 1))
        for n in range(2):
            for h in range(2):
                relays[2 * n + h].wait_recv()
                seen(n, (h, 2))

    gather(((at(ws[0], 0), z_ring), (at(ws[1], 0), y_ring)), lambda n, what: None)
    other = []

    def forward(n, what):
        h, slot = what
        other.append(send(ws[n][h].at[slot], ws[n][h].at[slot], partner))

    for n in range(2):
        for h in range(2):
            forward(n, (h, 0))
    gather(((ws[0], y_ring), (ws[1], z_ring)), forward)
    for copy in other:
        copy.wait_recv()

    for core in range(2):
        for (first, second), (u0, u1) in zip(PAIRS[core], ((w00, w01), (w10, w11))):
            swap = u0 is w10
            place_in = 0
            for b in (first, second):
                for i in range(16):
                    dy, dz = lax.rem(i // 4 + 4 - y, 4), lax.rem(i % 4 + 4 - z, 4)
                    one, two = (dz, dy) if swap else (dy, dz)
                    for t in range(8 - b):
                        n = place_in + t
                        value = u0[core, one, two, n] if n < FIRST else u1[core, one, two, n - FIRST]
                        gram_ref[BLOCK * b + 8 * i:BLOCK * b + 8 * i + 8, BLOCK * (b + t):BLOCK * (b + t + 1)] = value
                place_in += 8 - b
    row = lax.broadcasted_iota(jnp.int32, (BLOCK, BLOCK), 0)
    col = lax.broadcasted_iota(jnp.int32, (BLOCK, BLOCK), 1)
    diagonal = jnp.zeros((BLOCK, BLOCK), jnp.float32)
    for b in range(8):
        diagonal += jnp.where(row == col, gram_ref[BLOCK * b:BLOCK * b + BLOCK, BLOCK * b:BLOCK * b + BLOCK], 0.0)
    norm = jnp.sqrt(jnp.sum(diagonal, keepdims=True)) + 1e-07
    scale = 1.0 / norm
    start_ref[...] = bb[0:OWN] * scale
    square = scale * scale
    for b in range(8):
        for t in range(b, 8):
            lanes = slice(BLOCK * t, BLOCK * t + BLOCK)
            rows = slice(BLOCK * b, BLOCK * b + BLOCK)
            value = gram_ref[rows, lanes] * square
            gram_ref[rows, lanes] = value
            if t > b:
                gram_ref[lanes, rows] = value.T
    for copy in started:
        copy.wait_send()


COPIES2 = 13 + 2 + 24 + 24 + 16


def gram_of(grads, momentum, count):
    part = ((FIRST, 8, BLOCK), (9 - FIRST, 8, BLOCK))
    f32 = jnp.float32
    both_parts = lambda *lead: [pltpu.VMEM(lead + p, f32) for p in part]
    vmem = pl.BlockSpec(memory_space=pltpu.VMEM)
    return pl.pallas_call(
        functools.partial(gram_kernel, count),
        out_shape=(jax.ShapeDtypeStruct((OWN, HID), f32), jax.ShapeDtypeStruct((OWN, HID), f32), jax.ShapeDtypeStruct((HID, HID), f32)),
        in_specs=[vmem] * 2,
        out_specs=[vmem] * 3,
        scratch_shapes=[
            pltpu.VMEM((8, 8, BLOCK), f32), pltpu.VMEM((4, 8, BLOCK), f32), pltpu.VMEM((4, 8, BLOCK), f32),
            pltpu.VMEM((2, OWN, HID), f32), pltpu.VMEM((2 * OWN, HID), f32),
            *both_parts(4, 4), *both_parts(4, 4),
            *both_parts(2, 3, 4), *both_parts(2, 4), *both_parts(2, 3),
            *both_parts(2, 4, 4), *both_parts(2, 4, 4),
            pltpu.SemaphoreType.DMA((COPIES2,)), pltpu.SemaphoreType.DMA((COPIES2,)),
        ],
        compiler_params=pltpu.CompilerParams(collective_id=1, has_side_effects=True, vmem_limit_bytes=60 << 20),
        name="reduce_gram",
    )(grads, momentum)


first_coef = 3.4445
second_coef = -4.775
third_coef = 2.0315
TILE = 256


def newton_schulz_kernel(gram_ref, start_ref, new_ref, out_ref, kept_ref, mats, left_ref, gram1_ref):
    kept_ref[...] = new_ref[...]

    def dot(left, right):
        return jnp.dot(left, right, preferred_element_type=jnp.float32)

    def keep(n, rows, lanes, value):
        high, low = halves(value)
        mats[n, 0, rows, lanes] = high
        mats[n, 1, rows, lanes] = low

    def cut(i):
        return slice(TILE * i, TILE * i + TILE)

    def product(left, right, new, base_ref, alpha, beta, new_ref):
        for r in range(4):
            high = mats[left, 0, cut(r), :]
            both = jnp.concatenate([high, mats[left, 1, cut(r), :]], axis=0)
            for q in range(r, 4):
                value = dot(both, mats[right, 0, :, cut(q)])
                value = value[:TILE] + (value[TILE:] + dot(high, mats[right, 1, :, cut(q)]))
                value = alpha * base_ref[cut(r), cut(q)] + beta * value
                keep(new, cut(r), cut(q), value)
                if new_ref is not None:
                    new_ref[cut(r), cut(q)] = value
                if q > r:
                    turned = value.T
                    keep(new, cut(q), cut(r), turned)
                    if new_ref is not None:
                        new_ref[cut(q), cut(r)] = turned

    def apply(value, n):
        high, low = halves(value)
        both = jnp.concatenate([high, low], axis=0)
        parts = []
        for q in range(4):
            part = dot(both, mats[n, 0, :, cut(q)])
            parts.append(part[:OWN] + (part[OWN:] + dot(high, mats[n, 1, :, cut(q)])))
        return jnp.concatenate(parts, axis=1)

    for i in range(4):
        keep(0, cut(i), slice(None), gram_ref[cut(i), :])
    product(0, 0, 1, gram_ref, second_coef, third_coef, None)
    iterate = start_ref[...]
    iterate = first_coef * iterate + apply(iterate, 1)
    product(0, 1, 2, gram_ref, first_coef, 1.0, left_ref)
    product(2, 1, 3, left_ref, first_coef, 1.0, gram1_ref)
    product(3, 3, 4, gram1_ref, second_coef, third_coef, None)

    def step1(value):
        return first_coef * value + apply(value, 4)

    def gram2(value):
        return step1(apply(step1(value), 3))

    iterate = step1(iterate)
    twice = second_coef * iterate + third_coef * gram2(iterate)
    iterate = first_coef * iterate + gram2(twice)
    out_ref[...] = iterate * (0.2 * math.sqrt(max(HID, WID)))


def newton_schulz(gram, start, new_momentum):
    f32 = jnp.float32
    vmem = pl.BlockSpec(memory_space=pltpu.VMEM)
    return pl.pallas_call(
        newton_schulz_kernel,
        out_shape=[jax.ShapeDtypeStruct((OWN, HID), f32)] * 2,
        in_specs=[vmem] * 3,
        out_specs=[vmem] * 2,
        scratch_shapes=[pltpu.VMEM((5, 2, HID, HID), jnp.bfloat16), pltpu.VMEM((HID, HID), f32), pltpu.VMEM((HID, HID), f32)],
        compiler_params=pltpu.CompilerParams(vmem_limit_bytes=60 << 20),
        name="newton_schulz",
    )(gram, start, new_momentum)


def body(local_grads, momentum):
    grads = reduce_scatter(local_grads[0, 0])
    count = HID * WID * lax.axis_size("expert")
    new_momentum, start, gram = gram_of(grads, momentum[0].T, count)
    update, new_momentum = newton_schulz(gram, start, new_momentum)
    return (new_momentum.T[None], update.T[None])


def solution(mesh):
    finer = Mesh(mesh.devices.reshape(4, 4, 2, mesh.shape["expert"]), DP_EXPERT)
    in_specs = (P("expert", DP, None, None), P("expert", None, DP))
    out_specs = (P("expert", None, DP), P("expert", None, DP))
    return jax.shard_map(body, mesh=finer, in_specs=in_specs, out_specs=out_specs, check_vma=False)
```

```python
import functools
import math

import jax
import jax.numpy as jnp
from jax import lax
from jax.experimental import pallas as pl
from jax.experimental.pallas import tpu as pltpu
from jax.sharding import Mesh
from jax.sharding import PartitionSpec as P

MESH = pl.DeviceIdType.MESH
HID, WID = 1024, 3584
OWN = WID // 32
HALF = OWN // 2
LANES = HID // 2
ORDER = (2, 1, 3, 0)
DP = ("dp_0", "dp_1", "dp_2")
DP_EXPERT = DP + ("expert",)


momentum_decay = 0.95
BLOCK = 128
PAIRS = (((0, 7), (3, 4)), ((1, 6), (2, 5)))
FIRST = 5
COPIES = 76 + 22 + 2 + 60 + 60 + 16


def halves(value):
    high = value.astype(jnp.bfloat16)
    return high, (value - high.astype(jnp.float32)).astype(jnp.bfloat16)


def place():
    return [lax.axis_index(a) for a in ("dp_0", "dp_1", "dp_2", "expert")]


def gram_kernel(count, x_hbm, m_hbm, new_ref, start_ref, gram_ref, raw, flat, mine, pa, pb, ra, rb, qa, qb, r2, both_g, both_m, s1, s2, bb, a0, a1, b0, b1, r0, r1, q0, q1, t0, t1, w00, w01, w10, w11, load_sem, send_sem, recv_sem):
    y, z, c, x = place()
    partner = (y, z, 1 - c, x)
    y_next, y_prev = (lax.rem(y + 1, 4), z, c, x), (lax.rem(y + 3, 4), z, c, x)
    z_next, z_prev = (y, lax.rem(z + 1, 4), c, x), (y, lax.rem(z + 3, 4), c, x)
    loads = []
    for k in range(4):
        first = pl.multiple_of(lax.rem(y + ORDER[k], 4) * 896, 128)
        load = pltpu.make_async_copy(x_hbm.at[:, pl.ds(first, 896)], raw.at[k], load_sem.at[k])
        load.start()
        loads.append(load)
    load = pltpu.make_async_copy(m_hbm, both_m.at[0], load_sem.at[4])
    load.start()
    loads.append(load)
    line = x * 2 + c
    x_line = [(y, z, lax.rem(lax.rem(line + d, 8), 2), lax.rem(line + d, 8) // 2) for d in range(1, 8)]
    spot = y * 4 + z
    plane = [(lax.rem(spot + d, 16) // 4, lax.rem(lax.rem(spot + d, 16), 4), c, x) for d in range(1, 16)]
    barrier = pltpu.get_barrier_semaphore()
    for peer in x_line + plane:
        pl.semaphore_signal(barrier, inc=1, device_id=peer, device_id_type=MESH)

    started = []

    def send(src, dst, peer):
        n = len(started)
        copy = pltpu.make_async_remote_copy(
            src_ref=src, dst_ref=dst, send_sem=send_sem.at[n], recv_sem=recv_sem.at[n],
            device_id=peer, device_id_type=MESH)
        copy.start()
        started.append(copy)
        return copy

    row = lax.broadcasted_iota(jnp.int32, (128, 128), 0)
    col = lax.broadcasted_iota(jnp.int32, (128, 128), 1)
    eye = jnp.where(row == col, 1.0, 0.0).astype(jnp.bfloat16)

    def turn(k):
        loads[k].wait()
        for b in range(7):
            flat[k, 128 * b:128 * b + 128, :] = lax.dot_general(
                eye, raw[k, :, 128 * b:128 * b + 128], (((1,), (1,)), ((), ())),
                preferred_element_type=jnp.float32)

    def rows_of(j, core):
        return pl.multiple_of((lax.rem(z + ORDER[j], 4) * 2 + core) * OWN, 8)

    pair = {}

    def exchange(k):
        for j in range(4):
            pair[k, j] = send(flat.at[k, pl.ds(rows_of(j, 1 - c), OWN)], mine.at[k, j], partner)

    def pair_sum(k):
        for j in range(4):
            pair[k, j].wait_recv()
            base = rows_of(j, c)
            for h in range(2):
                lanes = slice(LANES * h, LANES * h + LANES)
                pa[k, j, h] = flat[k, pl.ds(base, HALF), lanes] + mine[k, j, 0:HALF, lanes]
                pb[j, k, h] = flat[k, pl.ds(base + HALF, HALF), lanes] + mine[k, j, HALF:OWN, lanes]

    def relay(p, r, nxt, prv):
        return [send(p(0, 0), r.at[0], nxt), send(p(0, 1), r.at[1], prv)]

    def unmerged_next(p, r, nxt):
        return send(p(1, 1), r.at[2], nxt)

    def unmerged_prev(p, r, prv):
        return send(p(2, 0), r.at[3], prv)

    def merged(p, r, nxt, prv, relays):
        relays[0].wait_recv()
        p(1, 0)[...] += r[0]
        first = send(p(1, 0), r.at[4], nxt)
        relays[1].wait_recv()
        p(2, 1)[...] += r[1]
        return [first, send(p(2, 1), r.at[5], prv)]

    def total(p, r, parts):
        for part in parts:
            part.wait_recv()
        return p(3, 0)[...] + r[4] + r[3], p(3, 1)[...] + r[2] + r[5]

    a_slots = [lambda s, h, j=j: pa.at[s, j, h] for j in range(4)]
    b_slots = [lambda s, h, k=k: pb.at[s, k, h] for k in range(4)]
    a_sent, b_sent = [[] for _ in range(4)], [[] for _ in range(4)]
    a_relay, b_relay = [None] * 4, [None] * 4

    def launch(k):
        pair_sum(k)
        b_relay[k] = relay(b_slots[k], rb.at[k], z_next, z_prev)
        if k == 0:
            for j in range(4):
                a_relay[j] = relay(a_slots[j], ra.at[j], y_next, y_prev)
        b_sent[k] += [unmerged_next(b_slots[k], rb.at[k], z_next), unmerged_prev(b_slots[k], rb.at[k], z_prev)]
        if k == 1:
            for j in range(4):
                a_sent[j].append(unmerged_next(a_slots[j], ra.at[j], y_next))
        if k == 2:
            for j in range(4):
                a_sent[j].append(unmerged_prev(a_slots[j], ra.at[j], y_prev))

    turn(0)
    pl.semaphore_wait(barrier, 22)
    exchange(0)
    turn(1)
    exchange(1)
    loads[4].wait()
    pair_m = send(both_m.at[0], both_m.at[1], partner)
    launch(0)
    turn(2)
    exchange(2)
    launch(1)
    turn(3)
    exchange(3)
    launch(2)
    launch(3)
    for i in range(4):
        a_sent[i] += merged(a_slots[i], ra.at[i], y_next, y_prev, a_relay[i])
        b_sent[i] += merged(b_slots[i], rb.at[i], z_next, z_prev, b_relay[i])

    last_a, last_b = (lambda s, h: qa.at[s, h]), (lambda s, h: qb.at[s, h])
    a_last, b_last = [], []
    for i in range(4):
        for q, slots, r, sent in ((qa, a_slots, ra, a_sent), (qb, b_slots, rb, b_sent)):
            q[i, 0], q[i, 1] = total(slots[i], r.at[i], sent[i])
        for last, r, nxt, prv, kept in ((last_a, r2.at[0], z_next, z_prev, a_last), (last_b, r2.at[1], y_next, y_prev, b_last)):
            if i == 0:
                kept.append(relay(last, r, nxt, prv))
            if i == 1:
                kept.append(unmerged_next(last, r, nxt))
            if i == 2:
                kept.append(unmerged_prev(last, r, prv))
    a_last += merged(last_a, r2.at[0], z_next, z_prev, a_last[0])
    b_last += merged(last_b, r2.at[1], y_next, y_prev, b_last[0])
    out = both_g.at[0]
    out[0:HALF, 0:LANES], out[0:HALF, LANES:HID] = total(last_a, r2.at[0], a_last[1:])
    out[HALF:OWN, 0:LANES], out[HALF:OWN, LANES:HID] = total(last_b, r2.at[1], b_last[1:])
    square = out[0:8, :] * out[0:8, :]
    for i in range(1, OWN // 8):
        square += out[8 * i:8 * i + 8, :] * out[8 * i:8 * i + 8, :]
    tile = square[:, 0:128]
    for i in range(1, 8):
        tile += square[:, 128 * i:128 * i + 128]
    for buf, own, peers in ((s1, line, x_line), (s2, spot, plane)):
        buf[own] = tile
        copies = [send(buf.at[own], buf.at[own], peer) for peer in peers]
        if buf is s1:
            pair_g = send(out, both_g.at[1], partner)
        for copy in copies:
            copy.wait_recv()
        tile = buf[0]
        for i in range(1, buf.shape[0]):
            tile += buf[i]
    root_mean = jnp.sqrt(jnp.sum(tile, keepdims=True) / count + 1e-06)
    factor = jnp.minimum(1.0, 1.0 / root_mean)
    clipped = factor * out[...]
    new = momentum_decay * both_m[0] + clipped
    new_ref[...] = new
    blend = clipped + momentum_decay * new
    bb[0:OWN] = blend
    pair_g.wait_recv()
    pair_m.wait_recv()
    clipped = factor * both_g[1]
    bb[OWN:2 * OWN] = clipped + momentum_decay * (momentum_decay * both_m[1] + clipped)
    high, low = halves(bb[...])
    turned = bb[...].T
    turned_high, turned_low = halves(turned)

    def dot(left, right):
        return jnp.dot(left, right, preferred_element_type=jnp.float32)

    for core in range(2):
        @pl.when(c == core)
        def _(core=core):
            for (first, second), (u0, u1) in zip(PAIRS[core], ((a0, a1), (b0, b1))):
                swap = u0 is b0
                place_in = 0
                for b in (first, second):
                    lh, ll = turned_high[BLOCK * b:BLOCK * b + BLOCK], turned_low[BLOCK * b:BLOCK * b + BLOCK]
                    rh, rl = high[:, BLOCK * b:], low[:, BLOCK * b:]
                    rows = dot(lh, rh) + (dot(lh, rl) + dot(ll, rh))
                    for i in range(16):
                        dy, dz = lax.rem(i // 4 + 4 - y, 4), lax.rem(i % 4 + 4 - z, 4)
                        one, two = (dz, dy) if swap else (dy, dz)
                        for t in range(8 - b):
                            value = rows[8 * i:8 * i + 8, BLOCK * t:BLOCK * t + BLOCK]
                            n = place_in + t
                            if n < FIRST:
                                u0[one, two, n] = value
                            else:
                                u1[one, two, n - FIRST] = value
                    place_in += 8 - b

    y_far, z_far = (lax.rem(y + 2, 4), z, c, x), (y, lax.rem(z + 2, 4), c, x)
    y_ring, z_ring = {1: y_next, 2: y_far, 3: y_prev}, {1: z_next, 2: z_far, 3: z_prev}
    colours = ((0, (a0, a1), y_ring, z_ring), (1, (b0, b1), z_ring, y_ring))
    far_first = (2, 1, 3, 0)
    relays, parts, lasts = {}, {}, [[], []]
    for s in far_first:
        for n, p, ring, _ in colours:
            relays[n, s] = [send(p[0].at[2, s], r0.at[n, 0, s], ring[1]), send(p[1].at[2, s], r1.at[n, 0, s], ring[3])]
    for s in far_first:
        for n, p, ring, _ in colours:
            parts[n, s] = [send(p[1].at[1, s], r1.at[n, 1, s], ring[1]), send(p[0].at[3, s], r0.at[n, 1, s], ring[3])]
    for s in far_first:
        for n, p, ring, _ in colours:
            relays[n, s][0].wait_recv()
            p[0][1, s] += r0[n, 0, s]
            parts[n, s].append(send(p[0].at[1, s], r0.at[n, 2, s], ring[1]))
            relays[n, s][1].wait_recv()
            p[1][3, s] += r1[n, 0, s]
            parts[n, s].append(send(p[1].at[3, s], r1.at[n, 2, s], ring[3]))
    for s in far_first:
        for n, p, _, ring in colours:
            for copy in parts[n, s]:
                copy.wait_recv()
            q0[n, s] = p[0][0, s] + r0[n, 1, s] + r0[n, 2, s]
            q1[n, s] = p[1][0, s] + r1[n, 1, s] + r1[n, 2, s]
            if s > 0:
                lasts[n] += [send(q0.at[n, s], t0.at[n, s], ring[s]), send(q1.at[n, s], t1.at[n, s], ring[s])]

    ws = ((w00.at[c], w01.at[c]), (w10.at[c], w11.at[c]))
    came, ring_parts, ring_relays, other = {}, {}, {}, []
    for n, _, _, ring in colours:
        for copy in lasts[n]:
            copy.wait_recv()
        ws[n][0][0, 0] = q0[n, 0] + t0[n, 1] + t0[n, 2] + t0[n, 3]
        ws[n][1][0, 0] = q1[n, 0] + t1[n, 1] + t1[n, 2] + t1[n, 3]
        for d in (2, 1, 3):
            came[n, 4 - d] = [send(w.at[0, 0], w.at[0, 4 - d], ring[d]) for w in ws[n]]

    def around(n, s):
        ring, (u0, u1) = colours[n][2], ws[n]
        ring_parts[n, s] = [
            send(u0.at[0, s], u0.at[3, s], ring[1]), send(u1.at[0, s], u1.at[1, s], ring[3]),
            send(u1.at[0, s], u1.at[3, s], ring[1]), send(u0.at[0, s], u0.at[1, s], ring[3])]

    def pass_on(n, s):
        ring, (u0, u1) = colours[n][2], ws[n]
        ring_parts[n, s][0].wait_recv()
        first = send(u0.at[3, s], u0.at[2, s], ring[1])
        ring_parts[n, s][1].wait_recv()
        ring_relays[n, s] = [first, send(u1.at[1, s], u1.at[2, s], ring[3])]

    def forward(n, slot):
        for w in ws[n]:
            other.append(send(w.at[slot], w.at[slot], partner))

    for n in range(2):
        around(n, 0)
    for s in (1, 3, 2):
        for n in range(2):
            for copy in came[n, s]:
                copy.wait_recv()
            around(n, s)
        if s == 3:
            for n in range(2):
                pass_on(n, 0)
    for n in range(2):
        forward(n, 0)
    for s in (1, 3, 2):
        for n in range(2):
            pass_on(n, s)
    for n in range(2):
        for s in range(4):
            ring_parts[n, s][2].wait_recv()
            ring_parts[n, s][3].wait_recv()
        forward(n, 1)
        forward(n, 3)
    for n in range(2):
        for s in range(4):
            for copy in ring_relays[n, s]:
                copy.wait_recv()
        forward(n, 2)
    for copy in other:
        copy.wait_recv()

    for core in range(2):
        for (first, second), (u0, u1) in zip(PAIRS[core], ((w00, w01), (w10, w11))):
            swap = u0 is w10
            place_in = 0
            for b in (first, second):
                for i in range(16):
                    dy, dz = lax.rem(i // 4 + 4 - y, 4), lax.rem(i % 4 + 4 - z, 4)
                    one, two = (dz, dy) if swap else (dy, dz)
                    for t in range(8 - b):
                        n = place_in + t
                        value = u0[core, one, two, n] if n < FIRST else u1[core, one, two, n - FIRST]
                        gram_ref[BLOCK * b + 8 * i:BLOCK * b + 8 * i + 8, BLOCK * (b + t):BLOCK * (b + t + 1)] = value
                place_in += 8 - b
    row = lax.broadcasted_iota(jnp.int32, (BLOCK, BLOCK), 0)
    col = lax.broadcasted_iota(jnp.int32, (BLOCK, BLOCK), 1)
    diagonal = jnp.zeros((BLOCK, BLOCK), jnp.float32)
    for b in range(8):
        diagonal += jnp.where(row == col, gram_ref[BLOCK * b:BLOCK * b + BLOCK, BLOCK * b:BLOCK * b + BLOCK], 0.0)
    norm = jnp.sqrt(jnp.sum(diagonal, keepdims=True)) + 1e-07
    scale = 1.0 / norm
    start_ref[...] = bb[0:OWN] * scale
    square = scale * scale
    for b in range(8):
        for t in range(b, 8):
            lanes = slice(BLOCK * t, BLOCK * t + BLOCK)
            rows = slice(BLOCK * b, BLOCK * b + BLOCK)
            value = gram_ref[rows, lanes] * square
            gram_ref[rows, lanes] = value
            if t > b:
                gram_ref[lanes, rows] = value.T
    for copy in started:
        copy.wait_send()


def gram_of(local, momentum, count):
    f32 = jnp.float32
    piece = (HALF, LANES)
    cut = ((FIRST, 8, BLOCK), (9 - FIRST, 8, BLOCK))

    def scratch(*lead):
        return [pltpu.VMEM(lead + p, f32) for p in cut]

    vmem = pl.BlockSpec(memory_space=pltpu.VMEM)
    return pl.pallas_call(
        functools.partial(gram_kernel, count),
        out_shape=(jax.ShapeDtypeStruct((OWN, HID), f32), jax.ShapeDtypeStruct((OWN, HID), f32), jax.ShapeDtypeStruct((HID, HID), f32)),
        in_specs=[pl.BlockSpec(memory_space=pl.ANY)] * 2,
        out_specs=[vmem] * 3,
        scratch_shapes=[
            pltpu.VMEM((4, HID, 896), jnp.bfloat16),
            pltpu.VMEM((4, 896, HID), f32),
            pltpu.VMEM((4, 4, OWN, HID), f32),
            pltpu.VMEM((4, 4, 2) + piece, f32), pltpu.VMEM((4, 4, 2) + piece, f32),
            pltpu.VMEM((4, 6) + piece, f32), pltpu.VMEM((4, 6) + piece, f32),
            pltpu.VMEM((4, 2) + piece, f32), pltpu.VMEM((4, 2) + piece, f32),
            pltpu.VMEM((2, 6) + piece, f32),
            pltpu.VMEM((2, OWN, HID), f32), pltpu.VMEM((2, OWN, HID), f32),
            pltpu.VMEM((8, 8, BLOCK), f32), pltpu.VMEM((16, 8, BLOCK), f32),
            pltpu.VMEM((2 * OWN, HID), f32),
            *scratch(4, 4), *scratch(4, 4), *scratch(2, 3, 4), *scratch(2, 4), *scratch(2, 4),
            *scratch(2, 4, 4), *scratch(2, 4, 4),
            pltpu.SemaphoreType.DMA((5,)),
            pltpu.SemaphoreType.DMA((COPIES,)), pltpu.SemaphoreType.DMA((COPIES,)),
        ],
        compiler_params=pltpu.CompilerParams(collective_id=0, has_side_effects=True, vmem_limit_bytes=63 << 20),
        name="gram_of_sum",
    )(local, momentum)


first_coef = 3.4445
second_coef = -4.775
third_coef = 2.0315
TILE = 256


def newton_schulz_kernel(gram_ref, start_ref, new_ref, out_ref, kept_ref, mats, left_ref, gram1_ref):
    kept_ref[...] = new_ref[...]

    def dot(left, right):
        return jnp.dot(left, right, preferred_element_type=jnp.float32)

    def keep(n, rows, lanes, value):
        high, low = halves(value)
        mats[n, 0, rows, lanes] = high
        mats[n, 1, rows, lanes] = low

    def cut(i):
        return slice(TILE * i, TILE * i + TILE)

    def product(left, right, new, base_ref, alpha, beta, new_ref):
        for r in range(4):
            high = mats[left, 0, cut(r), :]
            both = jnp.concatenate([high, mats[left, 1, cut(r), :]], axis=0)
            for q in range(r, 4):
                value = dot(both, mats[right, 0, :, cut(q)])
                value = value[:TILE] + (value[TILE:] + dot(high, mats[right, 1, :, cut(q)]))
                value = alpha * base_ref[cut(r), cut(q)] + beta * value
                keep(new, cut(r), cut(q), value)
                if new_ref is not None:
                    new_ref[cut(r), cut(q)] = value
                if q > r:
                    turned = value.T
                    keep(new, cut(q), cut(r), turned)
                    if new_ref is not None:
                        new_ref[cut(q), cut(r)] = turned

    def apply(value, n):
        high, low = halves(value)
        both = jnp.concatenate([high, low], axis=0)
        parts = []
        for q in range(4):
            part = dot(both, mats[n, 0, :, cut(q)])
            parts.append(part[:OWN] + (part[OWN:] + dot(high, mats[n, 1, :, cut(q)])))
        return jnp.concatenate(parts, axis=1)

    for i in range(4):
        keep(0, cut(i), slice(None), gram_ref[cut(i), :])
    product(0, 0, 1, gram_ref, second_coef, third_coef, None)
    iterate = start_ref[...]
    iterate = first_coef * iterate + apply(iterate, 1)
    product(0, 1, 2, gram_ref, first_coef, 1.0, left_ref)
    product(2, 1, 3, left_ref, first_coef, 1.0, gram1_ref)
    product(3, 3, 4, gram1_ref, second_coef, third_coef, None)

    def step1(value):
        return first_coef * value + apply(value, 4)

    def gram2(value):
        return step1(apply(step1(value), 3))

    iterate = step1(iterate)
    twice = second_coef * iterate + third_coef * gram2(iterate)
    iterate = first_coef * iterate + gram2(twice)
    out_ref[...] = iterate * (0.2 * math.sqrt(max(HID, WID)))


def newton_schulz(gram, start, new_momentum):
    f32 = jnp.float32
    vmem = pl.BlockSpec(memory_space=pltpu.VMEM)
    return pl.pallas_call(
        newton_schulz_kernel,
        out_shape=[jax.ShapeDtypeStruct((OWN, HID), f32)] * 2,
        in_specs=[vmem] * 3,
        out_specs=[vmem] * 2,
        scratch_shapes=[pltpu.VMEM((5, 2, HID, HID), jnp.bfloat16), pltpu.VMEM((HID, HID), f32), pltpu.VMEM((HID, HID), f32)],
        compiler_params=pltpu.CompilerParams(vmem_limit_bytes=60 << 20),
        name="newton_schulz",
    )(gram, start, new_momentum)


def body(local_grads, momentum):
    count = HID * WID * lax.axis_size("expert")
    new_momentum, start, gram = gram_of(local_grads[0, 0], momentum[0].T, count)
    update, new_momentum = newton_schulz(gram, start, new_momentum)
    return (new_momentum.T[None], update.T[None])


def solution(mesh):
    finer = Mesh(mesh.devices.reshape(4, 4, 2, mesh.shape["expert"]), DP_EXPERT)
    in_specs = (P("expert", DP, None, None), P("expert", None, DP))
    out_specs = (P("expert", None, DP), P("expert", None, DP))
    return jax.shard_map(body, mesh=finer, in_specs=in_specs, out_specs=out_specs, check_vma=False)
```

```python
import functools
import math

import jax
import jax.numpy as jnp
from jax import lax
from jax.experimental import pallas as pl
from jax.experimental.pallas import tpu as pltpu
from jax.sharding import Mesh
from jax.sharding import PartitionSpec as P

MESH = pl.DeviceIdType.MESH
HID, WID = 1024, 3584
OWN = WID // 32
HALF = OWN // 2
LANES = HID // 2
ORDER = (2, 1, 3, 0)
DP = ("dp_0", "dp_1", "dp_2")
DP_EXPERT = DP + ("expert",)


momentum_decay = 0.95
BLOCK = 128
PAIRS = (((0, 7), (3, 4)), ((1, 6), (2, 5)))
FIRST = 5
COPIES = 76 + 22 + 2 + 60 + 60 + 64


def halves(value):
    high = value.astype(jnp.bfloat16)
    return high, (value - high.astype(jnp.float32)).astype(jnp.bfloat16)


def place():
    return [lax.axis_index(a) for a in ("dp_0", "dp_1", "dp_2", "expert")]


def gram_kernel(count, x_hbm, m_hbm, new_ref, start_ref, gram_ref, raw, flat, mine, pa, pb, ra, rb, qa, qb, r2, both_g, both_m, s1, s2, bb, a0, a1, b0, b1, r0, r1, q0, q1, t0, t1, w00, w01, w10, w11, load_sem, send_sem, recv_sem):
    y, z, c, x = place()
    partner = (y, z, 1 - c, x)
    y_next, y_prev = (lax.rem(y + 1, 4), z, c, x), (lax.rem(y + 3, 4), z, c, x)
    z_next, z_prev = (y, lax.rem(z + 1, 4), c, x), (y, lax.rem(z + 3, 4), c, x)
    loads = []
    for k in range(4):
        first = pl.multiple_of(lax.rem(y + ORDER[k], 4) * 896, 128)
        load = pltpu.make_async_copy(x_hbm.at[:, pl.ds(first, 896)], raw.at[k], load_sem.at[k])
        load.start()
        loads.append(load)
    load = pltpu.make_async_copy(m_hbm, both_m.at[0], load_sem.at[4])
    load.start()
    loads.append(load)
    line = x * 2 + c
    x_line = [(y, z, lax.rem(lax.rem(line + d, 8), 2), lax.rem(line + d, 8) // 2) for d in range(1, 8)]
    spot = y * 4 + z
    plane = [(lax.rem(spot + d, 16) // 4, lax.rem(lax.rem(spot + d, 16), 4), c, x) for d in range(1, 16)]
    barrier = pltpu.get_barrier_semaphore()
    for peer in x_line + plane:
        pl.semaphore_signal(barrier, inc=1, device_id=peer, device_id_type=MESH)

    started = []

    def send(src, dst, peer):
        n = len(started)
        copy = pltpu.make_async_remote_copy(
            src_ref=src, dst_ref=dst, send_sem=send_sem.at[n], recv_sem=recv_sem.at[n],
            device_id=peer, device_id_type=MESH)
        copy.start()
        started.append(copy)
        return copy

    row = lax.broadcasted_iota(jnp.int32, (128, 128), 0)
    col = lax.broadcasted_iota(jnp.int32, (128, 128), 1)
    eye = jnp.where(row == col, 1.0, 0.0).astype(jnp.bfloat16)

    def turn(k):
        loads[k].wait()
        for b in range(7):
            flat[k, 128 * b:128 * b + 128, :] = lax.dot_general(
                eye, raw[k, :, 128 * b:128 * b + 128], (((1,), (1,)), ((), ())),
                preferred_element_type=jnp.float32)

    def rows_of(j, core):
        return pl.multiple_of((lax.rem(z + ORDER[j], 4) * 2 + core) * OWN, 8)

    pair = {}

    def exchange(k):
        for j in range(4):
            pair[k, j] = send(flat.at[k, pl.ds(rows_of(j, 1 - c), OWN)], mine.at[k, j], partner)

    def pair_sum(k, j):
        pair[k, j].wait_recv()
        base = rows_of(j, c)
        for h in range(2):
            lanes = slice(LANES * h, LANES * h + LANES)
            pa[k, j, h] = flat[k, pl.ds(base, HALF), lanes] + mine[k, j, 0:HALF, lanes]
            pb[j, k, h] = flat[k, pl.ds(base + HALF, HALF), lanes] + mine[k, j, HALF:OWN, lanes]

    def relay(p, r, nxt, prv):
        return [send(p(0, 0), r.at[0], nxt), send(p(0, 1), r.at[1], prv)]

    def unmerged_next(p, r, nxt):
        return send(p(1, 1), r.at[2], nxt)

    def unmerged_prev(p, r, prv):
        return send(p(2, 0), r.at[3], prv)

    def merged(p, r, nxt, prv, relays):
        relays[0].wait_recv()
        p(1, 0)[...] += r[0]
        first = send(p(1, 0), r.at[4], nxt)
        relays[1].wait_recv()
        p(2, 1)[...] += r[1]
        return [first, send(p(2, 1), r.at[5], prv)]

    def total(p, r, parts):
        for part in parts:
            part.wait_recv()
        return p(3, 0)[...] + r[4] + r[3], p(3, 1)[...] + r[2] + r[5]

    a_slots = [lambda s, h, j=j: pa.at[s, j, h] for j in range(4)]
    b_slots = [lambda s, h, k=k: pb.at[s, k, h] for k in range(4)]
    a_sent, b_sent = [[] for _ in range(4)], [[] for _ in range(4)]
    a_relay, b_relay = [None] * 4, [None] * 4

    def launch(k):
        for j in range(4):
            pair_sum(k, j)
            if k == 0:
                a_relay[j] = relay(a_slots[j], ra.at[j], y_next, y_prev)
            if k == 1:
                a_sent[j].append(unmerged_next(a_slots[j], ra.at[j], y_next))
            if k == 2:
                a_sent[j].append(unmerged_prev(a_slots[j], ra.at[j], y_prev))
            if j == 0:
                b_relay[k] = relay(b_slots[k], rb.at[k], z_next, z_prev)
            if j == 1:
                b_sent[k].append(unmerged_next(b_slots[k], rb.at[k], z_next))
            if j == 2:
                b_sent[k].append(unmerged_prev(b_slots[k], rb.at[k], z_prev))

    turn(0)
    pl.semaphore_wait(barrier, 22)
    exchange(0)
    turn(1)
    exchange(1)
    launch(0)
    turn(2)
    exchange(2)
    launch(1)
    turn(3)
    exchange(3)
    loads[4].wait()
    pair_m = send(both_m.at[0], both_m.at[1], partner)
    launch(2)
    launch(3)
    for i in range(4):
        a_sent[i] += merged(a_slots[i], ra.at[i], y_next, y_prev, a_relay[i])
        b_sent[i] += merged(b_slots[i], rb.at[i], z_next, z_prev, b_relay[i])

    last_a, last_b = (lambda s, h: qa.at[s, h]), (lambda s, h: qb.at[s, h])
    a_last, b_last = [], []
    for i in range(4):
        for q, slots, r, sent in ((qa, a_slots, ra, a_sent), (qb, b_slots, rb, b_sent)):
            q[i, 0], q[i, 1] = total(slots[i], r.at[i], sent[i])
        for last, r, nxt, prv, kept in ((last_a, r2.at[0], z_next, z_prev, a_last), (last_b, r2.at[1], y_next, y_prev, b_last)):
            if i == 0:
                kept.append(relay(last, r, nxt, prv))
            if i == 1:
                kept.append(unmerged_next(last, r, nxt))
            if i == 2:
                kept.append(unmerged_prev(last, r, prv))
    a_last += merged(last_a, r2.at[0], z_next, z_prev, a_last[0])
    b_last += merged(last_b, r2.at[1], y_next, y_prev, b_last[0])
    out = both_g.at[0]
    out[0:HALF, 0:LANES], out[0:HALF, LANES:HID] = total(last_a, r2.at[0], a_last[1:])
    out[HALF:OWN, 0:LANES], out[HALF:OWN, LANES:HID] = total(last_b, r2.at[1], b_last[1:])
    square = out[0:8, :] * out[0:8, :]
    for i in range(1, OWN // 8):
        square += out[8 * i:8 * i + 8, :] * out[8 * i:8 * i + 8, :]
    tile = square[:, 0:128]
    for i in range(1, 8):
        tile += square[:, 128 * i:128 * i + 128]
    for buf, own, peers in ((s1, line, x_line), (s2, spot, plane)):
        buf[own] = tile
        copies = [send(buf.at[own], buf.at[own], peer) for peer in peers]
        if buf is s1:
            pair_g = send(out, both_g.at[1], partner)
        for copy in copies:
            copy.wait_recv()
        tile = buf[0]
        for i in range(1, buf.shape[0]):
            tile += buf[i]
    root_mean = jnp.sqrt(jnp.sum(tile, keepdims=True) / count + 1e-06)
    factor = jnp.minimum(1.0, 1.0 / root_mean)
    clipped = factor * out[...]
    new = momentum_decay * both_m[0] + clipped
    new_ref[...] = new
    blend = clipped + momentum_decay * new
    bb[0:OWN] = blend
    pair_g.wait_recv()
    pair_m.wait_recv()
    clipped = factor * both_g[1]
    bb[OWN:2 * OWN] = clipped + momentum_decay * (momentum_decay * both_m[1] + clipped)
    high, low = halves(bb[...])
    turned = bb[...].T
    turned_high, turned_low = halves(turned)

    def dot(left, right):
        return jnp.dot(left, right, preferred_element_type=jnp.float32)

    for core in range(2):
        @pl.when(c == core)
        def _(core=core):
            for (first, second), (u0, u1) in zip(PAIRS[core], ((a0, a1), (b0, b1))):
                swap = u0 is b0
                place_in = 0
                for b in (first, second):
                    lh, ll = turned_high[BLOCK * b:BLOCK * b + BLOCK], turned_low[BLOCK * b:BLOCK * b + BLOCK]
                    rh, rl = high[:, BLOCK * b:], low[:, BLOCK * b:]
                    rows = dot(lh, rh) + (dot(lh, rl) + dot(ll, rh))
                    for i in range(16):
                        dy, dz = lax.rem(i // 4 + 4 - y, 4), lax.rem(i % 4 + 4 - z, 4)
                        one, two = (dz, dy) if swap else (dy, dz)
                        for t in range(8 - b):
                            value = rows[8 * i:8 * i + 8, BLOCK * t:BLOCK * t + BLOCK]
                            n = place_in + t
                            if n < FIRST:
                                u0[one, two, n] = value
                            else:
                                u1[one, two, n - FIRST] = value
                    place_in += 8 - b

    y_far, z_far = (lax.rem(y + 2, 4), z, c, x), (y, lax.rem(z + 2, 4), c, x)
    y_ring, z_ring = {1: y_next, 2: y_far, 3: y_prev}, {1: z_next, 2: z_far, 3: z_prev}
    colours = ((0, (a0, a1), y_ring, z_ring), (1, (b0, b1), z_ring, y_ring))
    far_first = (2, 1, 3, 0)
    relays, parts, lasts = {}, {}, [[], []]
    for s in far_first:
        for n, p, ring, _ in colours:
            relays[n, s] = [send(p[0].at[2, s], r0.at[n, 0, s], ring[1]), send(p[1].at[2, s], r1.at[n, 0, s], ring[3])]
    for s in far_first:
        for n, p, ring, _ in colours:
            parts[n, s] = [send(p[1].at[1, s], r1.at[n, 1, s], ring[1]), send(p[0].at[3, s], r0.at[n, 1, s], ring[3])]
    for s in far_first:
        for n, p, ring, _ in colours:
            relays[n, s][0].wait_recv()
            p[0][1, s] += r0[n, 0, s]
            parts[n, s].append(send(p[0].at[1, s], r0.at[n, 2, s], ring[1]))
            relays[n, s][1].wait_recv()
            p[1][3, s] += r1[n, 0, s]
            parts[n, s].append(send(p[1].at[3, s], r1.at[n, 2, s], ring[3]))
    for s in far_first:
        for n, p, _, ring in colours:
            for copy in parts[n, s]:
                copy.wait_recv()
            q0[n, s] = p[0][0, s] + r0[n, 1, s] + r0[n, 2, s]
            q1[n, s] = p[1][0, s] + r1[n, 1, s] + r1[n, 2, s]
            if s > 0:
                lasts[n] += [send(q0.at[n, s], t0.at[n, s], ring[s]), send(q1.at[n, s], t1.at[n, s], ring[s])]

    ws = ((w00.at[c], w01.at[c]), (w10.at[c], w11.at[c]))
    came, spread, other = {}, {}, []
    for n, _, _, ring in colours:
        for copy in lasts[n]:
            copy.wait_recv()
        ws[n][0][0, 0] = q0[n, 0] + t0[n, 1] + t0[n, 2] + t0[n, 3]
        ws[n][1][0, 0] = q1[n, 0] + t1[n, 1] + t1[n, 2] + t1[n, 3]
        for d in (2, 1, 3):
            came[n, 4 - d] = [send(w.at[0, 0], w.at[0, 4 - d], ring[d]) for w in ws[n]]

    def around(n, s):
        for d in (2, 1, 3):
            spread[n, 4 - d, s] = [send(w.at[0, s], w.at[4 - d, s], colours[n][2][d]) for w in ws[n]]

    def forward(n, slot, s):
        for w in ws[n]:
            other.append(send(w.at[slot, s], w.at[slot, s], partner))

    for n in range(2):
        around(n, 0)
    for s in (1, 3, 2):
        for n in range(2):
            for copy in came[n, s]:
                copy.wait_recv()
            around(n, s)
    for s in range(4):
        for n in range(2):
            forward(n, 0, s)
    for s in (0, 1, 3, 2):
        for slot in (1, 3, 2):
            for n in range(2):
                for copy in spread[n, slot, s]:
                    copy.wait_recv()
                forward(n, slot, s)
    for copy in other:
        copy.wait_recv()

    for core in range(2):
        for (first, second), (u0, u1) in zip(PAIRS[core], ((w00, w01), (w10, w11))):
            swap = u0 is w10
            place_in = 0
            for b in (first, second):
                for i in range(16):
                    dy, dz = lax.rem(i // 4 + 4 - y, 4), lax.rem(i % 4 + 4 - z, 4)
                    one, two = (dz, dy) if swap else (dy, dz)
                    for t in range(8 - b):
                        n = place_in + t
                        value = u0[core, one, two, n] if n < FIRST else u1[core, one, two, n - FIRST]
                        gram_ref[BLOCK * b + 8 * i:BLOCK * b + 8 * i + 8, BLOCK * (b + t):BLOCK * (b + t + 1)] = value
                place_in += 8 - b
    row = lax.broadcasted_iota(jnp.int32, (BLOCK, BLOCK), 0)
    col = lax.broadcasted_iota(jnp.int32, (BLOCK, BLOCK), 1)
    diagonal = jnp.zeros((BLOCK, BLOCK), jnp.float32)
    for b in range(8):
        diagonal += jnp.where(row == col, gram_ref[BLOCK * b:BLOCK * b + BLOCK, BLOCK * b:BLOCK * b + BLOCK], 0.0)
    norm = jnp.sqrt(jnp.sum(diagonal, keepdims=True)) + 1e-07
    scale = 1.0 / norm
    start_ref[...] = bb[0:OWN] * scale
    square = scale * scale
    for b in range(8):
        for t in range(b, 8):
            lanes = slice(BLOCK * t, BLOCK * t + BLOCK)
            rows = slice(BLOCK * b, BLOCK * b + BLOCK)
            value = gram_ref[rows, lanes] * square
            gram_ref[rows, lanes] = value
            if t > b:
                gram_ref[lanes, rows] = value.T
    for copy in started:
        copy.wait_send()


def gram_of(local, momentum, count):
    f32 = jnp.float32
    piece = (HALF, LANES)
    cut = ((FIRST, 8, BLOCK), (9 - FIRST, 8, BLOCK))

    def scratch(*lead):
        return [pltpu.VMEM(lead + p, f32) for p in cut]

    vmem = pl.BlockSpec(memory_space=pltpu.VMEM)
    return pl.pallas_call(
        functools.partial(gram_kernel, count),
        out_shape=(jax.ShapeDtypeStruct((OWN, HID), f32), jax.ShapeDtypeStruct((OWN, HID), f32), jax.ShapeDtypeStruct((HID, HID), f32)),
        in_specs=[pl.BlockSpec(memory_space=pl.ANY)] * 2,
        out_specs=[vmem] * 3,
        scratch_shapes=[
            pltpu.VMEM((4, HID, 896), jnp.bfloat16),
            pltpu.VMEM((4, 896, HID), f32),
            pltpu.VMEM((4, 4, OWN, HID), f32),
            pltpu.VMEM((4, 4, 2) + piece, f32), pltpu.VMEM((4, 4, 2) + piece, f32),
            pltpu.VMEM((4, 6) + piece, f32), pltpu.VMEM((4, 6) + piece, f32),
            pltpu.VMEM((4, 2) + piece, f32), pltpu.VMEM((4, 2) + piece, f32),
            pltpu.VMEM((2, 6) + piece, f32),
            pltpu.VMEM((2, OWN, HID), f32), pltpu.VMEM((2, OWN, HID), f32),
            pltpu.VMEM((8, 8, BLOCK), f32), pltpu.VMEM((16, 8, BLOCK), f32),
            pltpu.VMEM((2 * OWN, HID), f32),
            *scratch(4, 4), *scratch(4, 4), *scratch(2, 3, 4), *scratch(2, 4), *scratch(2, 4),
            *scratch(2, 4, 4), *scratch(2, 4, 4),
            pltpu.SemaphoreType.DMA((5,)),
            pltpu.SemaphoreType.DMA((COPIES,)), pltpu.SemaphoreType.DMA((COPIES,)),
        ],
        compiler_params=pltpu.CompilerParams(collective_id=0, has_side_effects=True, vmem_limit_bytes=63 << 20),
        name="gram_of_sum",
    )(local, momentum)


first_coef = 3.4445
second_coef = -4.775
third_coef = 2.0315
TILE = 256


def newton_schulz_kernel(gram_ref, start_ref, new_ref, out_ref, kept_ref, mats, left_ref, gram1_ref):
    kept_ref[...] = new_ref[...]

    def dot(left, right):
        return jnp.dot(left, right, preferred_element_type=jnp.float32)

    def keep(n, rows, lanes, value):
        high, low = halves(value)
        mats[n, 0, rows, lanes] = high
        mats[n, 1, rows, lanes] = low

    def cut(i):
        return slice(TILE * i, TILE * i + TILE)

    def product(left, right, new, base_ref, alpha, beta, new_ref):
        for r in range(4):
            high = mats[left, 0, cut(r), :]
            both = jnp.concatenate([high, mats[left, 1, cut(r), :]], axis=0)
            for q in range(r, 4):
                value = dot(both, mats[right, 0, :, cut(q)])
                value = value[:TILE] + (value[TILE:] + dot(high, mats[right, 1, :, cut(q)]))
                value = alpha * base_ref[cut(r), cut(q)] + beta * value
                keep(new, cut(r), cut(q), value)
                if new_ref is not None:
                    new_ref[cut(r), cut(q)] = value
                if q > r:
                    turned = value.T
                    keep(new, cut(q), cut(r), turned)
                    if new_ref is not None:
                        new_ref[cut(q), cut(r)] = turned

    def apply(value, n):
        high, low = halves(value)
        both = jnp.concatenate([high, low], axis=0)
        parts = []
        for q in range(4):
            part = dot(both, mats[n, 0, :, cut(q)])
            parts.append(part[:OWN] + (part[OWN:] + dot(high, mats[n, 1, :, cut(q)])))
        return jnp.concatenate(parts, axis=1)

    for i in range(4):
        keep(0, cut(i), slice(None), gram_ref[cut(i), :])
    product(0, 0, 1, gram_ref, second_coef, third_coef, None)
    iterate = start_ref[...]
    iterate = first_coef * iterate + apply(iterate, 1)
    product(0, 1, 2, gram_ref, first_coef, 1.0, left_ref)
    product(2, 1, 3, left_ref, first_coef, 1.0, gram1_ref)
    product(3, 3, 4, gram1_ref, second_coef, third_coef, None)

    def step1(value):
        return first_coef * value + apply(value, 4)

    def gram2(value):
        return step1(apply(step1(value), 3))

    iterate = step1(iterate)
    twice = second_coef * iterate + third_coef * gram2(iterate)
    iterate = first_coef * iterate + gram2(twice)
    out_ref[...] = iterate * (0.2 * math.sqrt(max(HID, WID)))


def newton_schulz(gram, start, new_momentum):
    f32 = jnp.float32
    vmem = pl.BlockSpec(memory_space=pltpu.VMEM)
    return pl.pallas_call(
        newton_schulz_kernel,
        out_shape=[jax.ShapeDtypeStruct((OWN, HID), f32)] * 2,
        in_specs=[vmem] * 3,
        out_specs=[vmem] * 2,
        scratch_shapes=[pltpu.VMEM((5, 2, HID, HID), jnp.bfloat16), pltpu.VMEM((HID, HID), f32), pltpu.VMEM((HID, HID), f32)],
        compiler_params=pltpu.CompilerParams(vmem_limit_bytes=60 << 20),
        name="newton_schulz",
    )(gram, start, new_momentum)


def body(local_grads, momentum):
    count = HID * WID * lax.axis_size("expert")
    new_momentum, start, gram = gram_of(local_grads[0, 0], momentum[0].T, count)
    update, new_momentum = newton_schulz(gram, start, new_momentum)
    return (new_momentum.T[None], update.T[None])


def solution(mesh):
    finer = Mesh(mesh.devices.reshape(4, 4, 2, mesh.shape["expert"]), DP_EXPERT)
    in_specs = (P("expert", DP, None, None), P("expert", None, DP))
    out_specs = (P("expert", None, DP), P("expert", None, DP))
    return jax.shard_map(body, mesh=finer, in_specs=in_specs, out_specs=out_specs, check_vma=False)
```

```python
import functools
import math

import jax
import jax.numpy as jnp
from jax import lax
from jax.experimental import pallas as pl
from jax.experimental.pallas import tpu as pltpu
from jax.sharding import Mesh
from jax.sharding import PartitionSpec as P

MESH = pl.DeviceIdType.MESH
HID, WID = 1024, 3584
OWN = WID // 32
HALF = OWN // 2
LANES = HID // 2
ORDER = (2, 1, 3, 0)
DP = ("dp_0", "dp_1", "dp_2")
DP_EXPERT = DP + ("expert",)


momentum_decay = 0.95
BLOCK = 128
PAIRS = (((0, 7), (3, 4)), ((1, 6), (2, 5)))
FIRST = 5
COPIES = 76 + 22 + 2 + 60 + 60 + 64


def halves(value):
    high = value.astype(jnp.bfloat16)
    return high, (value - high.astype(jnp.float32)).astype(jnp.bfloat16)


def place():
    return [lax.axis_index(a) for a in ("dp_0", "dp_1", "dp_2", "expert")]


def gram_kernel(count, x_hbm, m_hbm, new_ref, start_ref, gram_ref, raw, flat, mine, pa, pb, ra, rb, qa, qb, r2, both_g, both_m, s1, s2, bb, a0, a1, b0, b1, r0, r1, q0, q1, t0, t1, w00, w01, w10, w11, load_sem, send_sem, recv_sem):
    y, z, c, x = place()
    partner = (y, z, 1 - c, x)
    y_next, y_prev = (lax.rem(y + 1, 4), z, c, x), (lax.rem(y + 3, 4), z, c, x)
    z_next, z_prev = (y, lax.rem(z + 1, 4), c, x), (y, lax.rem(z + 3, 4), c, x)
    loads = []
    for k in range(4):
        first = pl.multiple_of(lax.rem(y + ORDER[k], 4) * 896, 128)
        load = pltpu.make_async_copy(x_hbm.at[:, pl.ds(first, 896)], raw.at[k], load_sem.at[k])
        load.start()
        loads.append(load)
    load = pltpu.make_async_copy(m_hbm, both_m.at[0], load_sem.at[4])
    load.start()
    loads.append(load)
    line = x * 2 + c
    x_line = [(y, z, lax.rem(lax.rem(line + d, 8), 2), lax.rem(line + d, 8) // 2) for d in range(1, 8)]
    spot = y * 4 + z
    plane = [(lax.rem(spot + d, 16) // 4, lax.rem(lax.rem(spot + d, 16), 4), c, x) for d in range(1, 16)]
    barrier = pltpu.get_barrier_semaphore()
    for peer in x_line + [y_next, y_prev, z_next, z_prev]:
        pl.semaphore_signal(barrier, inc=1, device_id=peer, device_id_type=MESH)

    started = []

    def send(src, dst, peer):
        n = len(started)
        copy = pltpu.make_async_remote_copy(
            src_ref=src, dst_ref=dst, send_sem=send_sem.at[n], recv_sem=recv_sem.at[n],
            device_id=peer, device_id_type=MESH)
        copy.start()
        started.append(copy)
        return copy

    row = lax.broadcasted_iota(jnp.int32, (128, 128), 0)
    col = lax.broadcasted_iota(jnp.int32, (128, 128), 1)
    eye = jnp.where(row == col, 1.0, 0.0).astype(jnp.bfloat16)

    def turn(k):
        loads[k].wait()
        for b in range(7):
            flat[k, 128 * b:128 * b + 128, :] = lax.dot_general(
                eye, raw[k, :, 128 * b:128 * b + 128], (((1,), (1,)), ((), ())),
                preferred_element_type=jnp.float32)

    def rows_of(j, core):
        return pl.multiple_of((lax.rem(z + ORDER[j], 4) * 2 + core) * OWN, 8)

    pair = {}

    def exchange(k):
        for j in range(4):
            pair[k, j] = send(flat.at[k, pl.ds(rows_of(j, 1 - c), OWN)], mine.at[k, j], partner)

    def pair_sum(k, j):
        pair[k, j].wait_recv()
        base = rows_of(j, c)
        for h in range(2):
            lanes = slice(LANES * h, LANES * h + LANES)
            pa[k, j, h] = flat[k, pl.ds(base, HALF), lanes] + mine[k, j, 0:HALF, lanes]
            pb[j, k, h] = flat[k, pl.ds(base + HALF, HALF), lanes] + mine[k, j, HALF:OWN, lanes]

    def relay(p, r, nxt, prv):
        return [send(p(0, 0), r.at[0], nxt), send(p(0, 1), r.at[1], prv)]

    def unmerged_next(p, r, nxt):
        return send(p(1, 1), r.at[2], nxt)

    def unmerged_prev(p, r, prv):
        return send(p(2, 0), r.at[3], prv)

    def merged(p, r, nxt, prv, relays):
        relays[0].wait_recv()
        p(1, 0)[...] += r[0]
        first = send(p(1, 0), r.at[4], nxt)
        relays[1].wait_recv()
        p(2, 1)[...] += r[1]
        return [first, send(p(2, 1), r.at[5], prv)]

    def total(p, r, parts):
        for part in parts:
            part.wait_recv()
        return p(3, 0)[...] + r[4] + r[3], p(3, 1)[...] + r[2] + r[5]

    a_slots = [lambda s, h, j=j: pa.at[s, j, h] for j in range(4)]
    b_slots = [lambda s, h, k=k: pb.at[s, k, h] for k in range(4)]
    a_sent, b_sent = [[] for _ in range(4)], [[] for _ in range(4)]
    a_relay, b_relay = [None] * 4, [None] * 4

    def launch(k):
        for j in range(4):
            pair_sum(k, j)
            if k == 0:
                a_relay[j] = relay(a_slots[j], ra.at[j], y_next, y_prev)
            if k == 1:
                a_sent[j].append(unmerged_next(a_slots[j], ra.at[j], y_next))
            if k == 2:
                a_sent[j].append(unmerged_prev(a_slots[j], ra.at[j], y_prev))
            if j == 0:
                b_relay[k] = relay(b_slots[k], rb.at[k], z_next, z_prev)
            if j == 1:
                b_sent[k].append(unmerged_next(b_slots[k], rb.at[k], z_next))
            if j == 2:
                b_sent[k].append(unmerged_prev(b_slots[k], rb.at[k], z_prev))

    turn(0)
    pl.semaphore_wait(barrier, 11)
    exchange(0)
    turn(1)
    exchange(1)
    launch(0)
    turn(2)
    exchange(2)
    launch(1)
    turn(3)
    exchange(3)
    loads[4].wait()
    pair_m = send(both_m.at[0], both_m.at[1], partner)
    launch(2)
    launch(3)
    for i in range(4):
        a_sent[i] += merged(a_slots[i], ra.at[i], y_next, y_prev, a_relay[i])
        b_sent[i] += merged(b_slots[i], rb.at[i], z_next, z_prev, b_relay[i])

    last_a, last_b = (lambda s, h: qa.at[s, h]), (lambda s, h: qb.at[s, h])
    a_last, b_last = [], []
    for i in range(4):
        for q, slots, r, sent in ((qa, a_slots, ra, a_sent), (qb, b_slots, rb, b_sent)):
            q[i, 0], q[i, 1] = total(slots[i], r.at[i], sent[i])
        for last, r, nxt, prv, kept in ((last_a, r2.at[0], z_next, z_prev, a_last), (last_b, r2.at[1], y_next, y_prev, b_last)):
            if i == 0:
                kept.append(relay(last, r, nxt, prv))
            if i == 1:
                kept.append(unmerged_next(last, r, nxt))
            if i == 2:
                kept.append(unmerged_prev(last, r, prv))
    a_last += merged(last_a, r2.at[0], z_next, z_prev, a_last[0])
    b_last += merged(last_b, r2.at[1], y_next, y_prev, b_last[0])
    out = both_g.at[0]
    out[0:HALF, 0:LANES], out[0:HALF, LANES:HID] = total(last_a, r2.at[0], a_last[1:])
    out[HALF:OWN, 0:LANES], out[HALF:OWN, LANES:HID] = total(last_b, r2.at[1], b_last[1:])
    square = out[0:8, :] * out[0:8, :]
    for i in range(1, OWN // 8):
        square += out[8 * i:8 * i + 8, :] * out[8 * i:8 * i + 8, :]
    tile = square[:, 0:128]
    for i in range(1, 8):
        tile += square[:, 128 * i:128 * i + 128]
    for buf, own, peers in ((s1, line, x_line), (s2, spot, plane)):
        buf[own] = tile
        copies = [send(buf.at[own], buf.at[own], peer) for peer in peers]
        if buf is s1:
            pair_g = send(out, both_g.at[1], partner)
        for copy in copies:
            copy.wait_recv()
        tile = buf[0]
        for i in range(1, buf.shape[0]):
            tile += buf[i]
    root_mean = jnp.sqrt(jnp.sum(tile, keepdims=True) / count + 1e-06)
    factor = jnp.minimum(1.0, 1.0 / root_mean)
    clipped = factor * out[...]
    new = momentum_decay * both_m[0] + clipped
    new_ref[...] = new
    blend = clipped + momentum_decay * new
    bb[0:OWN] = blend
    pair_g.wait_recv()
    pair_m.wait_recv()
    clipped = factor * both_g[1]
    bb[OWN:2 * OWN] = clipped + momentum_decay * (momentum_decay * both_m[1] + clipped)
    high, low = halves(bb[...])
    turned = bb[...].T
    turned_high, turned_low = halves(turned)

    def dot(left, right):
        return jnp.dot(left, right, preferred_element_type=jnp.float32)

    for core in range(2):
        @pl.when(c == core)
        def _(core=core):
            for (first, second), (u0, u1) in zip(PAIRS[core], ((a0, a1), (b0, b1))):
                swap = u0 is b0
                place_in = 0
                for b in (first, second):
                    lh, ll = turned_high[BLOCK * b:BLOCK * b + BLOCK], turned_low[BLOCK * b:BLOCK * b + BLOCK]
                    rh, rl = high[:, BLOCK * b:], low[:, BLOCK * b:]
                    rows = dot(lh, rh) + (dot(lh, rl) + dot(ll, rh))
                    for i in range(16):
                        dy, dz = lax.rem(i // 4 + 4 - y, 4), lax.rem(i % 4 + 4 - z, 4)
                        one, two = (dz, dy) if swap else (dy, dz)
                        for t in range(8 - b):
                            value = rows[8 * i:8 * i + 8, BLOCK * t:BLOCK * t + BLOCK]
                            n = place_in + t
                            if n < FIRST:
                                u0[one, two, n] = value
                            else:
                                u1[one, two, n - FIRST] = value
                    place_in += 8 - b

    y_far, z_far = (lax.rem(y + 2, 4), z, c, x), (y, lax.rem(z + 2, 4), c, x)
    y_ring, z_ring = {1: y_next, 2: y_far, 3: y_prev}, {1: z_next, 2: z_far, 3: z_prev}
    colours = ((0, (a0, a1), y_ring, z_ring), (1, (b0, b1), z_ring, y_ring))
    far_first = (2, 1, 3, 0)
    relays, parts, lasts = {}, {}, [[], []]
    for s in far_first:
        for n, p, ring, _ in colours:
            relays[n, s] = [send(p[0].at[2, s], r0.at[n, 0, s], ring[1]), send(p[1].at[2, s], r1.at[n, 0, s], ring[3])]
    for s in far_first:
        for n, p, ring, _ in colours:
            parts[n, s] = [send(p[1].at[1, s], r1.at[n, 1, s], ring[1]), send(p[0].at[3, s], r0.at[n, 1, s], ring[3])]
    for s in far_first:
        for n, p, ring, _ in colours:
            relays[n, s][0].wait_recv()
            p[0][1, s] += r0[n, 0, s]
            parts[n, s].append(send(p[0].at[1, s], r0.at[n, 2, s], ring[1]))
            relays[n, s][1].wait_recv()
            p[1][3, s] += r1[n, 0, s]
            parts[n, s].append(send(p[1].at[3, s], r1.at[n, 2, s], ring[3]))
    for s in far_first:
        for n, p, _, ring in colours:
            for copy in parts[n, s]:
                copy.wait_recv()
            q0[n, s] = p[0][0, s] + r0[n, 1, s] + r0[n, 2, s]
            q1[n, s] = p[1][0, s] + r1[n, 1, s] + r1[n, 2, s]
            if s > 0:
                lasts[n] += [send(q0.at[n, s], t0.at[n, s], ring[s]), send(q1.at[n, s], t1.at[n, s], ring[s])]

    ws = ((w00.at[c], w01.at[c]), (w10.at[c], w11.at[c]))
    came, spread, other = {}, {}, []
    for n, _, _, ring in colours:
        for copy in lasts[n]:
            copy.wait_recv()
        ws[n][0][0, 0] = q0[n, 0] + t0[n, 1] + t0[n, 2] + t0[n, 3]
        ws[n][1][0, 0] = q1[n, 0] + t1[n, 1] + t1[n, 2] + t1[n, 3]
        for d in (2, 1, 3):
            came[n, 4 - d] = [send(w.at[0, 0], w.at[0, 4 - d], ring[d]) for w in ws[n]]

    def around(n, s):
        for d in (2, 1, 3):
            spread[n, 4 - d, s] = [send(w.at[0, s], w.at[4 - d, s], colours[n][2][d]) for w in ws[n]]

    def forward(n, slot, s):
        for w in ws[n]:
            other.append(send(w.at[slot, s], w.at[slot, s], partner))

    for n in range(2):
        around(n, 0)
    for s in (1, 3, 2):
        for n in range(2):
            for copy in came[n, s]:
                copy.wait_recv()
            around(n, s)
    for s in range(4):
        for n in range(2):
            forward(n, 0, s)
    for s in (0, 1, 3, 2):
        for slot in (1, 3, 2):
            for n in range(2):
                for copy in spread[n, slot, s]:
                    copy.wait_recv()
                forward(n, slot, s)
    for copy in other:
        copy.wait_recv()

    for core in range(2):
        for (first, second), (u0, u1) in zip(PAIRS[core], ((w00, w01), (w10, w11))):
            swap = u0 is w10
            place_in = 0
            for b in (first, second):
                for i in range(16):
                    dy, dz = lax.rem(i // 4 + 4 - y, 4), lax.rem(i % 4 + 4 - z, 4)
                    one, two = (dz, dy) if swap else (dy, dz)
                    for t in range(8 - b):
                        n = place_in + t
                        value = u0[core, one, two, n] if n < FIRST else u1[core, one, two, n - FIRST]
                        gram_ref[BLOCK * b + 8 * i:BLOCK * b + 8 * i + 8, BLOCK * (b + t):BLOCK * (b + t + 1)] = value
                place_in += 8 - b
    row = lax.broadcasted_iota(jnp.int32, (BLOCK, BLOCK), 0)
    col = lax.broadcasted_iota(jnp.int32, (BLOCK, BLOCK), 1)
    diagonal = jnp.zeros((BLOCK, BLOCK), jnp.float32)
    for b in range(8):
        diagonal += jnp.where(row == col, gram_ref[BLOCK * b:BLOCK * b + BLOCK, BLOCK * b:BLOCK * b + BLOCK], 0.0)
    norm = jnp.sqrt(jnp.sum(diagonal, keepdims=True)) + 1e-07
    scale = 1.0 / norm
    start_ref[...] = bb[0:OWN] * scale
    square = scale * scale
    for b in range(8):
        for t in range(b, 8):
            lanes = slice(BLOCK * t, BLOCK * t + BLOCK)
            rows = slice(BLOCK * b, BLOCK * b + BLOCK)
            value = gram_ref[rows, lanes] * square
            gram_ref[rows, lanes] = value
            if t > b:
                gram_ref[lanes, rows] = value.T
    for copy in started:
        copy.wait_send()


def gram_of(local, momentum, count):
    f32 = jnp.float32
    piece = (HALF, LANES)
    cut = ((FIRST, 8, BLOCK), (9 - FIRST, 8, BLOCK))

    def scratch(*lead):
        return [pltpu.VMEM(lead + p, f32) for p in cut]

    vmem = pl.BlockSpec(memory_space=pltpu.VMEM)
    return pl.pallas_call(
        functools.partial(gram_kernel, count),
        out_shape=(jax.ShapeDtypeStruct((OWN, HID), f32), jax.ShapeDtypeStruct((OWN, HID), f32), jax.ShapeDtypeStruct((HID, HID), f32)),
        in_specs=[pl.BlockSpec(memory_space=pl.ANY)] * 2,
        out_specs=[vmem] * 3,
        scratch_shapes=[
            pltpu.VMEM((4, HID, 896), jnp.bfloat16),
            pltpu.VMEM((4, 896, HID), f32),
            pltpu.VMEM((4, 4, OWN, HID), f32),
            pltpu.VMEM((4, 4, 2) + piece, f32), pltpu.VMEM((4, 4, 2) + piece, f32),
            pltpu.VMEM((4, 6) + piece, f32), pltpu.VMEM((4, 6) + piece, f32),
            pltpu.VMEM((4, 2) + piece, f32), pltpu.VMEM((4, 2) + piece, f32),
            pltpu.VMEM((2, 6) + piece, f32),
            pltpu.VMEM((2, OWN, HID), f32), pltpu.VMEM((2, OWN, HID), f32),
            pltpu.VMEM((8, 8, BLOCK), f32), pltpu.VMEM((16, 8, BLOCK), f32),
            pltpu.VMEM((2 * OWN, HID), f32),
            *scratch(4, 4), *scratch(4, 4), *scratch(2, 3, 4), *scratch(2, 4), *scratch(2, 4),
            *scratch(2, 4, 4), *scratch(2, 4, 4),
            pltpu.SemaphoreType.DMA((5,)),
            pltpu.SemaphoreType.DMA((COPIES,)), pltpu.SemaphoreType.DMA((COPIES,)),
        ],
        compiler_params=pltpu.CompilerParams(collective_id=0, has_side_effects=True, vmem_limit_bytes=63 << 20),
        name="gram_of_sum",
    )(local, momentum)


first_coef = 3.4445
second_coef = -4.775
third_coef = 2.0315
TILE = 256


def newton_schulz_kernel(gram_ref, start_ref, new_ref, out_ref, kept_ref, mats, left_ref, gram1_ref):
    kept_ref[...] = new_ref[...]

    def dot(left, right):
        return jnp.dot(left, right, preferred_element_type=jnp.float32)

    def keep(n, rows, lanes, value):
        high, low = halves(value)
        mats[n, 0, rows, lanes] = high
        mats[n, 1, rows, lanes] = low

    def cut(i):
        return slice(TILE * i, TILE * i + TILE)

    def product(left, right, new, base_ref, alpha, beta, new_ref):
        for r in range(4):
            high = mats[left, 0, cut(r), :]
            both = jnp.concatenate([high, mats[left, 1, cut(r), :]], axis=0)
            for q in range(r, 4):
                value = dot(both, mats[right, 0, :, cut(q)])
                value = value[:TILE] + (value[TILE:] + dot(high, mats[right, 1, :, cut(q)]))
                value = alpha * base_ref[cut(r), cut(q)] + beta * value
                keep(new, cut(r), cut(q), value)
                if new_ref is not None:
                    new_ref[cut(r), cut(q)] = value
                if q > r:
                    turned = value.T
                    keep(new, cut(q), cut(r), turned)
                    if new_ref is not None:
                        new_ref[cut(q), cut(r)] = turned

    def apply(value, n):
        high, low = halves(value)
        both = jnp.concatenate([high, low], axis=0)
        parts = []
        for q in range(4):
            part = dot(both, mats[n, 0, :, cut(q)])
            parts.append(part[:OWN] + (part[OWN:] + dot(high, mats[n, 1, :, cut(q)])))
        return jnp.concatenate(parts, axis=1)

    for i in range(4):
        keep(0, cut(i), slice(None), gram_ref[cut(i), :])
    product(0, 0, 1, gram_ref, second_coef, third_coef, None)
    iterate = start_ref[...]
    iterate = first_coef * iterate + apply(iterate, 1)
    product(0, 1, 2, gram_ref, first_coef, 1.0, left_ref)
    product(2, 1, 3, left_ref, first_coef, 1.0, gram1_ref)
    product(3, 3, 4, gram1_ref, second_coef, third_coef, None)

    def step1(value):
        return first_coef * value + apply(value, 4)

    def gram2(value):
        return step1(apply(step1(value), 3))

    iterate = step1(iterate)
    twice = second_coef * iterate + third_coef * gram2(iterate)
    iterate = first_coef * iterate + gram2(twice)
    out_ref[...] = iterate * (0.2 * math.sqrt(max(HID, WID)))


def newton_schulz(gram, start, new_momentum):
    f32 = jnp.float32
    vmem = pl.BlockSpec(memory_space=pltpu.VMEM)
    return pl.pallas_call(
        newton_schulz_kernel,
        out_shape=[jax.ShapeDtypeStruct((OWN, HID), f32)] * 2,
        in_specs=[vmem] * 3,
        out_specs=[vmem] * 2,
        scratch_shapes=[pltpu.VMEM((5, 2, HID, HID), jnp.bfloat16), pltpu.VMEM((HID, HID), f32), pltpu.VMEM((HID, HID), f32)],
        compiler_params=pltpu.CompilerParams(vmem_limit_bytes=60 << 20),
        name="newton_schulz",
    )(gram, start, new_momentum)


def body(local_grads, momentum):
    count = HID * WID * lax.axis_size("expert")
    new_momentum, start, gram = gram_of(local_grads[0, 0], momentum[0].T, count)
    update, new_momentum = newton_schulz(gram, start, new_momentum)
    return (new_momentum.T[None], update.T[None])


def solution(mesh):
    finer = Mesh(mesh.devices.reshape(4, 4, 2, mesh.shape["expert"]), DP_EXPERT)
    in_specs = (P("expert", DP, None, None), P("expert", None, DP))
    out_specs = (P("expert", None, DP), P("expert", None, DP))
    return jax.shard_map(body, mesh=finer, in_specs=in_specs, out_specs=out_specs, check_vma=False)
```
